256 devices in a mesh: dp: 16 (over y_hi, x, core), ctx: 16 (over z, y_lo).
Axes of the slice: x: 4, y: 4 (y_hi: 2, y_lo: 2; y = y_hi * 2 + y_lo), z: 8, core: 2. Of those that a mesh axis runs over, the one named last changes fastest.
Arguments:
- queries: bfloat16 [65536, 2048], P(('dp', 'ctx')), parts along dimension 0, may hold values from -6 to 6
- key_states: bfloat16 [65536, 512], P(('dp', 'ctx')), parts along dimension 0, may hold values from -6 to 6
- value_states: bfloat16 [65536, 512], P(('dp', 'ctx')), parts along dimension 0, may hold values from -6 to 6
- grad_output: bfloat16 [65536, 2048], P(('dp', 'ctx')), parts along dimension 0, may hold values from -30 to 30
- log_norms: float32 [16, 65536], P(None, ('dp', 'ctx')), parts along dimension 1, may hold values from 6 to 7.5
- grad_dots: float32 [16, 65536], P(None, ('dp', 'ctx')), parts along dimension 1, may hold values from -150 to 150
- block_routes: int32 [256, 4], P(('dp', 'ctx')), parts along dimension 0, may hold values from 0 to 15, as said below
- owner_steps: int32 [64], P('dp'), parts along dimension 0, may hold values from 0 to 15, as said below
Outputs:
- grad_queries: bfloat16 [65536, 2048], P(('dp', 'ctx')), parts along dimension 0
- grad_keys: bfloat16 [65536, 512], P(('dp', 'ctx')), parts along dimension 0
- grad_values: bfloat16 [65536, 512], P(('dp', 'ctx')), parts along dimension 0
The draws below stay inside these ranges and needn't reach their ends.
There are 16 independent parts, one for each index of `dp`. The reference program is written for one: setup_inputs(seed, part) draws one part's arguments, and reference() takes and returns one part's arrays. A program takes and returns all parts, laid end to end along the dimension named above; each array names one. Nothing has to cross between parts.
Inputs may be any that keep to these rules, and one draw needn't show every extreme that they name: block_routes[b, 0] = b; every entry of row b lies between 0 and b; entries of a row may repeat. `owner_steps`: 4 distinct indices of devices along ctx; device c along ctx holds block c.
All inputs are finite; a program needn't handle non-finite values.
Results may differ from the reference program's by a relative error of at most 0.0065.
Values may be sent and summed in bfloat16 or wider, within the bound.
A program may use at most 128 MiB of HBM per device.

```python
import math
import jax
import jax.numpy as jnp
from jax import lax

HQ = 16
HK = 4
DH = 128
BLK = 256
TOPK = 4
SEQ = 4096
BLOCKS = 16
BPD = 1
STEPS = 4


def draw_block_routes(key, part):
    rows = jnp.arange(BLOCKS, dtype=jnp.int32)
    key_first, key_second = jax.random.split(jax.random.fold_in(key, 11))
    upper = rows[:, None] + 1
    first = jax.random.randint(key_first, (BLOCKS, TOPK - 1), 0, upper)
    second = jax.random.randint(key_second, (BLOCKS, TOPK - 1), 0, upper)
    picks = jnp.minimum(first, second)
    return jnp.concatenate([rows[:, None], picks], axis=1).astype(jnp.int32)


def draw_owner_steps(key, part):
    count = BLOCKS // BPD
    key_high, key_low = jax.random.split(jax.random.fold_in(key, 23))
    high = jax.random.randint(key_high, (count,), 0, 4096, dtype=jnp.int32)
    low = jax.random.randint(key_low, (count,), 0, 4096, dtype=jnp.int32)
    ranks = jnp.arange(count, dtype=jnp.int32)
    scores = (high * 4096 + low) % 65536 * count + ranks
    order = jnp.argsort(-scores, stable=True)
    return order[:STEPS].astype(jnp.int32)


def block_scale(rng, extent, shards, low, top_value):
    factor_of, own = 1.0, jax.random.fold_in(rng, 6)
    for dim, blocks in shards:
        draws = jnp.exp(jax.random.uniform(jax.random.fold_in(own, dim), (blocks,), jnp.float32, low / len(shards), top_value / len(shards)))
        factor_of = factor_of * jnp.repeat(draws, extent[dim] // blocks).reshape([-1 if axis == dim else 1 for axis in range(len(extent))])
    return factor_of


def gaussian(stream_key, shape, deviation, most, shards=(), held_as=jnp.bfloat16):
    values = deviation * jax.random.normal(stream_key, shape, jnp.float32)
    if shards:
        values = values * block_scale(stream_key, shape, shards, -0.22, 0.18)
    return jnp.clip(values, -most, most).astype(held_as)


def setup_inputs(seed: int = 0, part: int = 0) -> dict:
    key_of = jax.random.split(jax.random.key(seed), 9)
    own_keys = jax.random.split(jax.random.fold_in(key_of[8], part), 9)
    return {
        "queries": gaussian(own_keys[0], (SEQ, HQ * DH), 1.0, 6.0, ((0, 16),)),
        "key_states": gaussian(own_keys[1], (SEQ, HK * DH), 1.0, 6.0, ((0, 16),)),
        "value_states": gaussian(own_keys[2], (SEQ, HK * DH), 1.0, 6.0, ((0, 16),)),
        "grad_output": jnp.clip(jax.random.uniform(own_keys[3], (SEQ, HQ * DH), jnp.float32, -30.0, 30.0) * block_scale(own_keys[3], (SEQ, HQ * DH), ((0, 16),), -0.4, 0.0), -30.0, 30.0).astype(jnp.bfloat16),
        "log_norms": jnp.clip(6.0 + 1.5 * jax.random.uniform(own_keys[4], (HQ, SEQ), jnp.float32) ** block_scale(own_keys[4], (HQ, SEQ), ((1, 16),), -0.2, 0.2), 6.0, 7.5),
        "grad_dots": jnp.clip(jax.random.uniform(own_keys[5], (HQ, SEQ), jnp.float32, -150.0, 150.0) * block_scale(own_keys[5], (HQ, SEQ), ((1, 16),), -0.4, 0.0), -150.0, 150.0),
        "block_routes": draw_block_routes(jax.random.fold_in(jax.random.fold_in(key_of[8], part), 71), part),
        "owner_steps": draw_owner_steps(jax.random.fold_in(jax.random.fold_in(key_of[8], part), 71), part),
    }


def pair_terms(query_rows, grad_rows, norm_rows, dot_rows, key_rows, value_rows, allowed):
    rows = query_rows.shape[0]
    cols = key_rows.shape[0]
    group = HQ // HK
    scale = 1.0 / math.sqrt(DH)
    query_heads = query_rows.astype(jnp.float32).reshape(rows, HK, group, DH)
    grad_heads = grad_rows.astype(jnp.float32).reshape(rows, HK, group, DH)
    key_heads = key_rows.astype(jnp.float32).reshape(cols, HK, DH)
    value_heads = value_rows.astype(jnp.float32).reshape(cols, HK, DH)
    scores = jnp.einsum('qhgd,khd->hgqk', query_heads, key_heads) * scale
    norms = norm_rows.reshape(HK, group, rows, 1)
    dots = dot_rows.reshape(HK, group, rows, 1)
    probs = jnp.where(allowed, jnp.exp(scores - norms), jnp.float32(0.0))
    grad_probs = jnp.einsum('qhgd,khd->hgqk', grad_heads, value_heads)
    grad_scores = lax.optimization_barrier((probs * (grad_probs - dots)).astype(jnp.bfloat16)).astype(jnp.float32)
    probs_low = lax.optimization_barrier(probs.astype(jnp.bfloat16)).astype(jnp.float32)
    grad_q = jnp.einsum('hgqk,khd->qhgd', grad_scores, key_heads).reshape(rows, HQ * DH) * scale
    grad_k = jnp.einsum('hgqk,qhgd->khd', grad_scores, query_heads).reshape(cols, HK * DH) * scale
    grad_v = jnp.einsum('hgqk,qhgd->khd', probs_low, grad_heads).reshape(cols, HK * DH)
    return (grad_q, grad_k, grad_v)

def reference(queries, key_states, value_states, grad_output, log_norms, grad_dots, block_routes, owner_steps):
    features = HK * DH
    positions = jnp.arange(BLK, dtype=jnp.int32)

    def one_block(carry, block):
        grad_k, grad_v = carry
        start = block * BLK
        query_rows = lax.dynamic_slice_in_dim(queries, start, BLK, 0)
        grad_rows = lax.dynamic_slice_in_dim(grad_output, start, BLK, 0)
        norm_rows = lax.dynamic_slice_in_dim(log_norms, start, BLK, 1)
        dot_rows = lax.dynamic_slice_in_dim(grad_dots, start, BLK, 1)
        listed = block_routes[block]
        grad_q = jnp.zeros((BLK, HQ * DH), jnp.float32)
        for slot in range(TOPK):
            target = listed[slot]
            if slot > 0:
                earlier = jnp.any(listed[:slot] == target)
            else:
                earlier = jnp.zeros((), jnp.bool_)
            covered = jnp.any(owner_steps == target // BPD)
            keep = jnp.logical_not(earlier) & ((target == block) | covered)
            key_start = (target * BLK).astype(jnp.int32)
            causal = key_start + positions[None, :] <= start + positions[:, None]
            allowed = causal & keep
            key_rows = lax.dynamic_slice_in_dim(key_states, key_start, BLK, 0)
            value_rows = lax.dynamic_slice_in_dim(value_states, key_start, BLK, 0)
            term_q, term_k, term_v = pair_terms(query_rows, grad_rows, norm_rows, dot_rows, key_rows, value_rows, allowed)
            grad_q = grad_q + term_q
            old_k = lax.dynamic_slice_in_dim(grad_k, key_start, BLK, 0)
            grad_k = lax.dynamic_update_slice_in_dim(grad_k, old_k + term_k, key_start, 0)
            old_v = lax.dynamic_slice_in_dim(grad_v, key_start, BLK, 0)
            grad_v = lax.dynamic_update_slice_in_dim(grad_v, old_v + term_v, key_start, 0)
        return ((grad_k, grad_v), grad_q.astype(jnp.bfloat16))
    empty = jnp.zeros((SEQ, features), jnp.float32)
    (grad_k, grad_v), grad_q = lax.scan(one_block, (empty, empty), jnp.arange(BLOCKS, dtype=jnp.int32))
    return (grad_q.reshape(SEQ, HQ * DH), grad_k.astype(jnp.bfloat16), grad_v.astype(jnp.bfloat16))
```

```python
import functools
import math

import jax
import jax.numpy as jnp
from jax import lax
from jax.experimental import pallas as pl
from jax.experimental.pallas import tpu as pltpu
from jax.sharding import PartitionSpec as P

HQ = 16
HK = 4
DH = 128
BLK = 256
MESH = pl.DeviceIdType.MESH


def ring_pos(c, n):
    y = c % 2
    z = c // 2
    return (1 - y) * z + y * (n - 1 - z)


def ring_ctx(p, n):
    q = p // (n // 2)
    return (1 - q) * (2 * p) + q * (2 * (n - 1 - p) + 1)


def ring_kernel(n, x_ref, o_ref, rbuf, rs_send, rs_recv, ag_send, ag_recv):
    me = lax.axis_index("ctx")
    row = lax.axis_index("dp")
    pos = ring_pos(me, n)
    right = ring_ctx((pos + 1) % n, n)
    left = ring_ctx((pos + n - 1) % n, n)
    peers = (right, left)

    barrier = pltpu.get_barrier_semaphore()
    for nb in (left, right):
        pl.semaphore_signal(barrier, inc=1, device_id=(row, nb), device_id_type=MESH)
    pl.semaphore_wait(barrier, 2)

    o_ref[...] = x_ref[...]

    def rs_copy(d, s):
        send = (pos + n - s) % n if d == 0 else (pos + s) % n
        return pltpu.make_async_remote_copy(
            src_ref=o_ref.at[d, send],
            dst_ref=rbuf.at[d, s],
            send_sem=rs_send.at[d, s],
            recv_sem=rs_recv.at[d, s],
            device_id=(row, peers[d]),
            device_id_type=MESH,
        )

    def rs_step(s, carry):
        copies = [rs_copy(d, s) for d in range(2)]
        for c in copies:
            c.start()
        for d in range(2):
            copies[d].wait_recv()
            got = (pos + 2 * n - s - 1) % n if d == 0 else (pos + s + 1) % n
            o_ref[d, got] = o_ref[d, got] + rbuf[d, s]
        for c in copies:
            c.wait_send()
        return carry

    lax.fori_loop(0, n - 1, rs_step, 0)

    def ag_copy(d, t):
        chunk = (pos + 1 + n - t) % n if d == 0 else (pos + n - 1 + t) % n
        return pltpu.make_async_remote_copy(
            src_ref=o_ref.at[d, chunk],
            dst_ref=o_ref.at[d, chunk],
            send_sem=ag_send.at[d, t],
            recv_sem=ag_recv.at[d, t],
            device_id=(row, peers[d]),
            device_id_type=MESH,
        )

    def ag_step(t, carry):
        copies = [ag_copy(d, t) for d in range(2)]
        for c in copies:
            c.start()
        for c in copies:
            c.wait_recv()
        for c in copies:
            c.wait_send()
        return carry

    lax.fori_loop(0, n - 1, ag_step, 0)


def ring_allreduce(x, n, cid):
    _, _, rows, cols = x.shape
    return pl.pallas_call(
        functools.partial(ring_kernel, n),
        out_shape=jax.ShapeDtypeStruct(x.shape, x.dtype),
        in_specs=[pl.BlockSpec(memory_space=pltpu.VMEM)],
        out_specs=pl.BlockSpec(memory_space=pltpu.VMEM),
        scratch_shapes=[
            pltpu.VMEM((2, n - 1, rows, cols), x.dtype),
            pltpu.SemaphoreType.DMA((2, n - 1)),
            pltpu.SemaphoreType.DMA((2, n - 1)),
            pltpu.SemaphoreType.DMA((2, n - 1)),
            pltpu.SemaphoreType.DMA((2, n - 1)),
        ],
        compiler_params=pltpu.CompilerParams(collective_id=cid, has_side_effects=True),
    )(x)


def slot_allreduce(slots, n, cid):
    steps, rows, cols = slots.shape
    total = steps * rows
    chunk = total // (2 * n)
    out = ring_allreduce(slots.reshape(2, n, chunk, cols), n, cid)
    return out.reshape(steps, rows, cols)


def pair_terms(query_rows, grad_rows, norm_rows, dot_rows, key_rows, value_rows, allowed):
    rows = query_rows.shape[0]
    cols = key_rows.shape[0]
    group = HQ // HK
    scale = 1.0 / math.sqrt(DH)
    query_heads = query_rows.reshape(rows, HK, group, DH)
    grad_heads = grad_rows.reshape(rows, HK, group, DH)
    key_heads = key_rows.reshape(cols, HK, DH)
    value_heads = value_rows.reshape(cols, HK, DH)
    scores = (
        jnp.einsum("qhgd,khd->hgqk", query_heads, key_heads, preferred_element_type=jnp.float32)
        * scale
    )
    norms = norm_rows.reshape(HK, group, rows, 1)
    dots = dot_rows.reshape(HK, group, rows, 1)
    probs = jnp.where(allowed, jnp.exp(scores - norms), jnp.float32(0.0))
    grad_probs = jnp.einsum(
        "qhgd,khd->hgqk", grad_heads, value_heads, preferred_element_type=jnp.float32
    )
    grad_scores = (probs * (grad_probs - dots)).astype(jnp.bfloat16)
    probs_low = probs.astype(jnp.bfloat16)
    grad_q = (
        jnp.einsum(
            "hgqk,khd->qhgd", grad_scores, key_heads, preferred_element_type=jnp.float32
        ).reshape(rows, HQ * DH)
        * scale
    )
    grad_k = (
        jnp.einsum(
            "hgqk,qhgd->khd", grad_scores, query_heads, preferred_element_type=jnp.float32
        ).reshape(cols, HK * DH)
        * scale
    )
    grad_v = jnp.einsum(
        "hgqk,qhgd->khd", probs_low, grad_heads, preferred_element_type=jnp.float32
    ).reshape(cols, HK * DH)
    return (grad_q, grad_k, grad_v)


def allowed_rows(local_routes, query_start, key_start, tokens, widen, active):
    per_dev = local_routes.shape[0]
    query_blocks = query_start // BLK + jnp.arange(per_dev, dtype=jnp.int32)
    key_blocks = key_start // BLK + jnp.arange(per_dev, dtype=jnp.int32)
    listed = jnp.any(local_routes[:, :, None] == key_blocks[None, None, :], axis=1)
    same = query_blocks[:, None] == key_blocks[None, :]
    chosen = listed & (same | widen) & active
    token_level = jnp.broadcast_to(chosen[:, None, :, None], (per_dev, BLK, per_dev, BLK)).reshape(
        tokens, tokens
    )
    positions = jnp.arange(tokens, dtype=jnp.int32)
    causal = key_start + positions[None, :] <= query_start + positions[:, None]
    return token_level & causal


def make_on_device(n):
    def on_device(
        queries, key_states, value_states, grad_output, log_norms, grad_dots, block_routes, owner_steps
    ):
        tokens = queries.shape[0]
        features = key_states.shape[1]
        device = lax.axis_index("ctx")
        start = device * tokens
        steps = owner_steps.shape[0]
        is_mine = owner_steps == device
        covered = jnp.any(is_mine)
        kv = jnp.concatenate([key_states, value_states], axis=1)
        kv_slots = jnp.where(is_mine[:, None, None], kv[None], jnp.zeros((), kv.dtype))
        kv_all = slot_allreduce(kv_slots, n, 0)
        local_mask = allowed_rows(block_routes, start, start, tokens, covered, jnp.ones((), jnp.bool_))
        grad_q, grad_k, grad_v = pair_terms(
            queries, grad_output, log_norms, grad_dots, key_states, value_states, local_mask
        )
        terms = []
        for step in range(steps):
            owner = owner_steps[step]
            key_part = kv_all[step, :, :features]
            value_part = kv_all[step, :, features:]
            step_mask = allowed_rows(
                block_routes, start, owner * tokens, tokens, jnp.ones((), jnp.bool_), owner != device
            )
            term_q, term_k, term_v = pair_terms(
                queries, grad_output, log_norms, grad_dots, key_part, value_part, step_mask
            )
            grad_q = grad_q + term_q
            terms.append(jnp.concatenate([term_k, term_v], axis=1))
        summed = slot_allreduce(jnp.stack(terms), n, 1)
        for step in range(steps):
            taken = is_mine[step]
            grad_k = grad_k + jnp.where(taken, summed[step, :, :features], jnp.float32(0.0))
            grad_v = grad_v + jnp.where(taken, summed[step, :, features:], jnp.float32(0.0))
        return (grad_q.astype(jnp.bfloat16), grad_k.astype(jnp.bfloat16), grad_v.astype(jnp.bfloat16))

    return on_device


def solution(mesh):
    n = mesh.shape["ctx"]
    return jax.shard_map(
        make_on_device(n),
        mesh=mesh,
        in_specs=(
            P(("dp", "ctx"), None),
            P(("dp", "ctx"), None),
            P(("dp", "ctx"), None),
            P(("dp", "ctx"), None),
            P(None, ("dp", "ctx")),
            P(None, ("dp", "ctx")),
            P(("dp", "ctx"), None),
            P("dp"),
        ),
        out_specs=(P(("dp", "ctx"), None), P(("dp", "ctx"), None), P(("dp", "ctx"), None)),
        check_vma=False,
    )
```

```python
import functools
import math

import jax
import jax.numpy as jnp
from jax import lax
from jax.experimental import pallas as pl
from jax.experimental.pallas import tpu as pltpu
from jax.sharding import PartitionSpec as P

HQ = 16
HK = 4
DH = 128
BLK = 256
MESH = pl.DeviceIdType.MESH


def direct_kernel(n, x_ref, o_ref, rbuf, rs_send, rs_recv, ag_send, ag_recv):
    me = lax.axis_index("ctx")
    row = lax.axis_index("dp")
    peers = [(me + k) % n for k in range(1, n)]

    barrier = pltpu.get_barrier_semaphore()
    for nb in peers:
        pl.semaphore_signal(barrier, inc=1, device_id=(row, nb), device_id_type=MESH)
    pl.semaphore_wait(barrier, n - 1)

    def rs_copy(nb):
        return pltpu.make_async_remote_copy(
            src_ref=x_ref.at[nb],
            dst_ref=rbuf.at[me],
            send_sem=rs_send.at[nb],
            recv_sem=rs_recv.at[me],
            device_id=(row, nb),
            device_id_type=MESH,
        )

    sends = [rs_copy(nb) for nb in peers]
    for c in sends:
        c.start()
    acc = x_ref[me].astype(jnp.float32)
    for nb in peers:
        pltpu.make_async_remote_copy(
            src_ref=x_ref.at[nb],
            dst_ref=rbuf.at[nb],
            send_sem=rs_send.at[nb],
            recv_sem=rs_recv.at[nb],
            device_id=(row, nb),
            device_id_type=MESH,
        ).wait_recv()
        acc = acc + rbuf[nb].astype(jnp.float32)
    o_ref[me] = acc.astype(o_ref.dtype)
    for c in sends:
        c.wait_send()

    def ag_copy(nb):
        return pltpu.make_async_remote_copy(
            src_ref=o_ref.at[me],
            dst_ref=o_ref.at[me],
            send_sem=ag_send.at[nb],
            recv_sem=ag_recv.at[me],
            device_id=(row, nb),
            device_id_type=MESH,
        )

    sends = [ag_copy(nb) for nb in peers]
    for c in sends:
        c.start()
    for nb in peers:
        pltpu.make_async_remote_copy(
            src_ref=o_ref.at[nb],
            dst_ref=o_ref.at[nb],
            send_sem=ag_send.at[nb],
            recv_sem=ag_recv.at[nb],
            device_id=(row, nb),
            device_id_type=MESH,
        ).wait_recv()
    for c in sends:
        c.wait_send()


def direct_allreduce(x, n, cid):
    _, rows, cols = x.shape
    return pl.pallas_call(
        functools.partial(direct_kernel, n),
        out_shape=jax.ShapeDtypeStruct(x.shape, x.dtype),
        in_specs=[pl.BlockSpec(memory_space=pltpu.VMEM)],
        out_specs=pl.BlockSpec(memory_space=pltpu.VMEM),
        scratch_shapes=[
            pltpu.VMEM((n, rows, cols), x.dtype),
            pltpu.SemaphoreType.DMA((n,)),
            pltpu.SemaphoreType.DMA((n,)),
            pltpu.SemaphoreType.DMA((n,)),
            pltpu.SemaphoreType.DMA((n,)),
        ],
        compiler_params=pltpu.CompilerParams(collective_id=cid, has_side_effects=True),
    )(x)


def slot_allreduce(slots, n, cid):
    steps, rows, cols = slots.shape
    total = steps * rows
    chunk = total // n
    out = direct_allreduce(slots.reshape(n, chunk, cols), n, cid)
    return out.reshape(steps, rows, cols)


def pair_terms(query_rows, grad_rows, norm_rows, dot_rows, key_rows, value_rows, allowed):
    rows = query_rows.shape[0]
    cols = key_rows.shape[0]
    group = HQ // HK
    scale = 1.0 / math.sqrt(DH)
    query_heads = query_rows.reshape(rows, HK, group, DH)
    grad_heads = grad_rows.reshape(rows, HK, group, DH)
    key_heads = key_rows.reshape(cols, HK, DH)
    value_heads = value_rows.reshape(cols, HK, DH)
    scores = (
        jnp.einsum("qhgd,khd->hgqk", query_heads, key_heads, preferred_element_type=jnp.float32)
        * scale
    )
    norms = norm_rows.reshape(HK, group, rows, 1)
    dots = dot_rows.reshape(HK, group, rows, 1)
    probs = jnp.where(allowed, jnp.exp(scores - norms), jnp.float32(0.0))
    grad_probs = jnp.einsum(
        "qhgd,khd->hgqk", grad_heads, value_heads, preferred_element_type=jnp.float32
    )
    grad_scores = (probs * (grad_probs - dots)).astype(jnp.bfloat16)
    probs_low = probs.astype(jnp.bfloat16)
    grad_q = (
        jnp.einsum(
            "hgqk,khd->qhgd", grad_scores, key_heads, preferred_element_type=jnp.float32
        ).reshape(rows, HQ * DH)
        * scale
    )
    grad_k = (
        jnp.einsum(
            "hgqk,qhgd->khd", grad_scores, query_heads, preferred_element_type=jnp.float32
        ).reshape(cols, HK * DH)
        * scale
    )
    grad_v = jnp.einsum(
        "hgqk,qhgd->khd", probs_low, grad_heads, preferred_element_type=jnp.float32
    ).reshape(cols, HK * DH)
    return (grad_q, grad_k, grad_v)


def allowed_rows(local_routes, query_start, key_start, tokens, widen, active):
    per_dev = local_routes.shape[0]
    query_blocks = query_start // BLK + jnp.arange(per_dev, dtype=jnp.int32)
    key_blocks = key_start // BLK + jnp.arange(per_dev, dtype=jnp.int32)
    listed = jnp.any(local_routes[:, :, None] == key_blocks[None, None, :], axis=1)
    same = query_blocks[:, None] == key_blocks[None, :]
    chosen = listed & (same | widen) & active
    token_level = jnp.broadcast_to(chosen[:, None, :, None], (per_dev, BLK, per_dev, BLK)).reshape(
        tokens, tokens
    )
    positions = jnp.arange(tokens, dtype=jnp.int32)
    causal = key_start + positions[None, :] <= query_start + positions[:, None]
    return token_level & causal


def make_on_device(n):
    def on_device(
        queries, key_states, value_states, grad_output, log_norms, grad_dots, block_routes, owner_steps
    ):
        tokens = queries.shape[0]
        features = key_states.shape[1]
        device = lax.axis_index("ctx")
        start = device * tokens
        steps = owner_steps.shape[0]
        is_mine = owner_steps == device
        covered = jnp.any(is_mine)
        kv = jnp.concatenate([key_states, value_states], axis=1)
        kv_slots = jnp.where(is_mine[:, None, None], kv[None], jnp.zeros((), kv.dtype))
        kv_all = slot_allreduce(kv_slots, n, 0)
        local_mask = allowed_rows(block_routes, start, start, tokens, covered, jnp.ones((), jnp.bool_))
        grad_q, grad_k, grad_v = pair_terms(
            queries, grad_output, log_norms, grad_dots, key_states, value_states, local_mask
        )
        terms = []
        for step in range(steps):
            owner = owner_steps[step]
            key_part = kv_all[step, :, :features]
            value_part = kv_all[step, :, features:]
            step_mask = allowed_rows(
                block_routes, start, owner * tokens, tokens, jnp.ones((), jnp.bool_), owner != device
            )
            term_q, term_k, term_v = pair_terms(
                queries, grad_output, log_norms, grad_dots, key_part, value_part, step_mask
            )
            grad_q = grad_q + term_q
            terms.append(jnp.concatenate([term_k, term_v], axis=1))
        summed = slot_allreduce(jnp.stack(terms), n, 1)
        for step in range(steps):
            taken = is_mine[step]
            grad_k = grad_k + jnp.where(taken, summed[step, :, :features], jnp.float32(0.0))
            grad_v = grad_v + jnp.where(taken, summed[step, :, features:], jnp.float32(0.0))
        return (grad_q.astype(jnp.bfloat16), grad_k.astype(jnp.bfloat16), grad_v.astype(jnp.bfloat16))

    return on_device


def solution(mesh):
    n = mesh.shape["ctx"]
    return jax.shard_map(
        make_on_device(n),
        mesh=mesh,
        in_specs=(
            P(("dp", "ctx"), None),
            P(("dp", "ctx"), None),
            P(("dp", "ctx"), None),
            P(("dp", "ctx"), None),
            P(None, ("dp", "ctx")),
            P(None, ("dp", "ctx")),
            P(("dp", "ctx"), None),
            P("dp"),
        ),
        out_specs=(P(("dp", "ctx"), None), P(("dp", "ctx"), None), P(("dp", "ctx"), None)),
        check_vma=False,
    )
```

```python
import functools
import math

import jax
import jax.numpy as jnp
from jax import lax
from jax.experimental import pallas as pl
from jax.experimental.pallas import tpu as pltpu
from jax.sharding import PartitionSpec as P

HQ = 16
HK = 4
DH = 128
BLK = 256
MESH = pl.DeviceIdType.MESH


def ring_pos(c, n):
    y = c % 2
    z = c // 2
    return (1 - y) * z + y * (n - 1 - z)


def ring_ctx(p, n):
    q = p // (n // 2)
    return (1 - q) * (2 * p) + q * (2 * (n - 1 - p) + 1)


def ring_kernel(n, x_ref, o_ref, rbuf, rs_send, rs_recv, ag_send, ag_recv, ready):
    me = lax.axis_index("ctx")
    row = lax.axis_index("dp")
    pos = ring_pos(me, n)
    right = ring_ctx((pos + 1) % n, n)
    left = ring_ctx((pos + n - 1) % n, n)
    peers = (right, left)

    barrier = pltpu.get_barrier_semaphore()
    for nb in (left, right):
        pl.semaphore_signal(barrier, inc=1, device_id=(row, nb), device_id_type=MESH)
    pl.semaphore_wait(barrier, 2)

    o_ref[...] = x_ref[...]

    def rs_copy(d, s):
        send = (pos + n - s) % n if d == 0 else (pos + s) % n
        return pltpu.make_async_remote_copy(
            src_ref=o_ref.at[d, send],
            dst_ref=rbuf.at[d, s],
            send_sem=rs_send.at[d, s],
            recv_sem=rs_recv.at[d, s],
            device_id=(row, peers[d]),
            device_id_type=MESH,
        )

    first = [rs_copy(d, 0) for d in range(2)]
    for c in first:
        c.start()

    def rs_step(s, carry):
        for d in range(2):
            rs_copy(d, s).wait_recv()
            got = (pos + 2 * n - s - 1) % n if d == 0 else (pos + s + 1) % n
            o_ref[d, got] = o_ref[d, got] + rbuf[d, s]

            @pl.when(s < n - 2)
            def _():
                rs_copy(d, s + 1).start()

        return carry

    lax.fori_loop(0, n - 1, rs_step, 0)

    def rs_drain(s, carry):
        for d in range(2):
            rs_copy(d, s).wait_send()
        return carry

    lax.fori_loop(0, n - 1, rs_drain, 0)
    for nb in (left, right):
        pl.semaphore_signal(ready, inc=1, device_id=(row, nb), device_id_type=MESH)
    pl.semaphore_wait(ready, 2)

    def ag_copy(d, t):
        chunk = (pos + 1 + n - t) % n if d == 0 else (pos + n - 1 + t) % n
        return pltpu.make_async_remote_copy(
            src_ref=o_ref.at[d, chunk],
            dst_ref=o_ref.at[d, chunk],
            send_sem=ag_send.at[d, t],
            recv_sem=ag_recv.at[d, t],
            device_id=(row, peers[d]),
            device_id_type=MESH,
        )

    first = [ag_copy(d, 0) for d in range(2)]
    for c in first:
        c.start()

    def ag_step(t, carry):
        for d in range(2):
            ag_copy(d, t).wait_recv()

            @pl.when(t < n - 2)
            def _():
                ag_copy(d, t + 1).start()

        return carry

    lax.fori_loop(0, n - 1, ag_step, 0)

    def drain(s, carry):
        for d in range(2):
            ag_copy(d, s).wait_send()
        return carry

    lax.fori_loop(0, n - 1, drain, 0)


def ring_allreduce(x, n, cid):
    _, _, rows, cols = x.shape
    return pl.pallas_call(
        functools.partial(ring_kernel, n),
        out_shape=jax.ShapeDtypeStruct(x.shape, x.dtype),
        in_specs=[pl.BlockSpec(memory_space=pltpu.VMEM)],
        out_specs=pl.BlockSpec(memory_space=pltpu.VMEM),
        scratch_shapes=[
            pltpu.VMEM((2, n - 1, rows, cols), x.dtype),
            pltpu.SemaphoreType.DMA((2, n - 1)),
            pltpu.SemaphoreType.DMA((2, n - 1)),
            pltpu.SemaphoreType.DMA((2, n - 1)),
            pltpu.SemaphoreType.DMA((2, n - 1)),
            pltpu.SemaphoreType.REGULAR,
        ],
        compiler_params=pltpu.CompilerParams(collective_id=cid, has_side_effects=True),
    )(x)


def slot_allreduce(slots, n, cid):
    steps, rows, cols = slots.shape
    total = steps * rows
    chunk = total // (2 * n)
    out = ring_allreduce(slots.reshape(2, n, chunk, cols), n, cid)
    return out.reshape(steps, rows, cols)


def pair_terms(query_rows, grad_rows, norm_rows, dot_rows, key_rows, value_rows, allowed):
    rows = query_rows.shape[0]
    cols = key_rows.shape[0]
    group = HQ // HK
    scale = 1.0 / math.sqrt(DH)
    query_heads = query_rows.reshape(rows, HK, group, DH)
    grad_heads = grad_rows.reshape(rows, HK, group, DH)
    key_heads = key_rows.reshape(cols, HK, DH)
    value_heads = value_rows.reshape(cols, HK, DH)
    scores = (
        jnp.einsum("qhgd,khd->hgqk", query_heads, key_heads, preferred_element_type=jnp.float32)
        * scale
    )
    norms = norm_rows.reshape(HK, group, rows, 1)
    dots = dot_rows.reshape(HK, group, rows, 1)
    probs = jnp.where(allowed, jnp.exp(scores - norms), jnp.float32(0.0))
    grad_probs = jnp.einsum(
        "qhgd,khd->hgqk", grad_heads, value_heads, preferred_element_type=jnp.float32
    )
    grad_scores = (probs * (grad_probs - dots)).astype(jnp.bfloat16)
    probs_low = probs.astype(jnp.bfloat16)
    grad_q = (
        jnp.einsum(
            "hgqk,khd->qhgd", grad_scores, key_heads, preferred_element_type=jnp.float32
        ).reshape(rows, HQ * DH)
        * scale
    )
    grad_k = (
        jnp.einsum(
            "hgqk,qhgd->khd", grad_scores, query_heads, preferred_element_type=jnp.float32
        ).reshape(cols, HK * DH)
        * scale
    )
    grad_v = jnp.einsum(
        "hgqk,qhgd->khd", probs_low, grad_heads, preferred_element_type=jnp.float32
    ).reshape(cols, HK * DH)
    return (grad_q, grad_k, grad_v)


def allowed_rows(local_routes, query_start, key_start, tokens, widen, active):
    per_dev = local_routes.shape[0]
    query_blocks = query_start // BLK + jnp.arange(per_dev, dtype=jnp.int32)
    key_blocks = key_start // BLK + jnp.arange(per_dev, dtype=jnp.int32)
    listed = jnp.any(local_routes[:, :, None] == key_blocks[None, None, :], axis=1)
    same = query_blocks[:, None] == key_blocks[None, :]
    chosen = listed & (same | widen) & active
    token_level = jnp.broadcast_to(chosen[:, None, :, None], (per_dev, BLK, per_dev, BLK)).reshape(
        tokens, tokens
    )
    positions = jnp.arange(tokens, dtype=jnp.int32)
    causal = key_start + positions[None, :] <= query_start + positions[:, None]
    return token_level & causal


def make_on_device(n):
    def on_device(
        queries, key_states, value_states, grad_output, log_norms, grad_dots, block_routes, owner_steps
    ):
        tokens = queries.shape[0]
        features = key_states.shape[1]
        device = lax.axis_index("ctx")
        start = device * tokens
        steps = owner_steps.shape[0]
        is_mine = owner_steps == device
        covered = jnp.any(is_mine)
        kv = jnp.concatenate([key_states, value_states], axis=1)
        kv_slots = jnp.where(is_mine[:, None, None], kv[None], jnp.zeros((), kv.dtype))
        kv_all = slot_allreduce(kv_slots, n, 0)
        local_mask = allowed_rows(block_routes, start, start, tokens, covered, jnp.ones((), jnp.bool_))
        grad_q, grad_k, grad_v = pair_terms(
            queries, grad_output, log_norms, grad_dots, key_states, value_states, local_mask
        )
        terms = []
        for step in range(steps):
            owner = owner_steps[step]
            key_part = kv_all[step, :, :features]
            value_part = kv_all[step, :, features:]
            step_mask = allowed_rows(
                block_routes, start, owner * tokens, tokens, jnp.ones((), jnp.bool_), owner != device
            )
            term_q, term_k, term_v = pair_terms(
                queries, grad_output, log_norms, grad_dots, key_part, value_part, step_mask
            )
            grad_q = grad_q + term_q
            terms.append(jnp.concatenate([term_k, term_v], axis=1))
        summed = slot_allreduce(jnp.stack(terms), n, 1)
        for step in range(steps):
            taken = is_mine[step]
            grad_k = grad_k + jnp.where(taken, summed[step, :, :features], jnp.float32(0.0))
            grad_v = grad_v + jnp.where(taken, summed[step, :, features:], jnp.float32(0.0))
        return (grad_q.astype(jnp.bfloat16), grad_k.astype(jnp.bfloat16), grad_v.astype(jnp.bfloat16))

    return on_device


def solution(mesh):
    n = mesh.shape["ctx"]
    return jax.shard_map(
        make_on_device(n),
        mesh=mesh,
        in_specs=(
            P(("dp", "ctx"), None),
            P(("dp", "ctx"), None),
            P(("dp", "ctx"), None),
            P(("dp", "ctx"), None),
            P(None, ("dp", "ctx")),
            P(None, ("dp", "ctx")),
            P(("dp", "ctx"), None),
            P("dp"),
        ),
        out_specs=(P(("dp", "ctx"), None), P(("dp", "ctx"), None), P(("dp", "ctx"), None)),
        check_vma=False,
    )
```

```python
import functools
import math

import jax
import jax.numpy as jnp
from jax import lax
from jax.experimental import pallas as pl
from jax.experimental.pallas import tpu as pltpu
from jax.sharding import PartitionSpec as P

HQ = 16
HK = 4
DH = 128
BLK = 256
MESH = pl.DeviceIdType.MESH


def ring_pos(c, n):
    y = c % 2
    z = c // 2
    return (1 - y) * z + y * (n - 1 - z)


def ring_ctx(p, n):
    q = p // (n // 2)
    return (1 - q) * (2 * p) + q * (2 * (n - 1 - p) + 1)


def ring_kernel(n, m, x_ref, o_ref, rbuf, rs_send, rs_recv, ag_send, ag_recv, ready):
    me = lax.axis_index("ctx")
    row = lax.axis_index("dp")
    pos = ring_pos(me, n)
    right = ring_ctx((pos + 1) % n, n)
    left = ring_ctx((pos + n - 1) % n, n)
    peers = (right, left)

    barrier = pltpu.get_barrier_semaphore()
    for nb in (left, right):
        pl.semaphore_signal(barrier, inc=1, device_id=(row, nb), device_id_type=MESH)
    pl.semaphore_wait(barrier, 2)

    o_ref[...] = x_ref[...]

    def rs_copy(d, s, k):
        send = (pos + n - s) % n if d == 0 else (pos + s) % n
        return pltpu.make_async_remote_copy(
            src_ref=o_ref.at[d, send, k],
            dst_ref=rbuf.at[d, s, k],
            send_sem=rs_send.at[d, s, k],
            recv_sem=rs_recv.at[d, s, k],
            device_id=(row, peers[d]),
            device_id_type=MESH,
        )

    for k in range(m):
        for d in range(2):
            rs_copy(d, 0, k).start()

    def rs_step(s, carry):
        for k in range(m):
            for d in range(2):
                rs_copy(d, s, k).wait_recv()
                got = (pos + 2 * n - s - 1) % n if d == 0 else (pos + s + 1) % n
                o_ref[d, got, k] = o_ref[d, got, k] + rbuf[d, s, k]

                @pl.when(s < n - 2)
                def _():
                    rs_copy(d, s + 1, k).start()

        return carry

    lax.fori_loop(0, n - 1, rs_step, 0)

    def rs_drain(s, carry):
        for k in range(m):
            for d in range(2):
                rs_copy(d, s, k).wait_send()
        return carry

    lax.fori_loop(0, n - 1, rs_drain, 0)
    for nb in (left, right):
        pl.semaphore_signal(ready, inc=1, device_id=(row, nb), device_id_type=MESH)
    pl.semaphore_wait(ready, 2)

    def ag_copy(d, t, k):
        chunk = (pos + 1 + n - t) % n if d == 0 else (pos + n - 1 + t) % n
        return pltpu.make_async_remote_copy(
            src_ref=o_ref.at[d, chunk, k],
            dst_ref=o_ref.at[d, chunk, k],
            send_sem=ag_send.at[d, t, k],
            recv_sem=ag_recv.at[d, t, k],
            device_id=(row, peers[d]),
            device_id_type=MESH,
        )

    for k in range(m):
        for d in range(2):
            ag_copy(d, 0, k).start()

    def ag_step(t, carry):
        for k in range(m):
            for d in range(2):
                ag_copy(d, t, k).wait_recv()

                @pl.when(t < n - 2)
                def _():
                    ag_copy(d, t + 1, k).start()

        return carry

    lax.fori_loop(0, n - 1, ag_step, 0)

    def drain(s, carry):
        for k in range(m):
            for d in range(2):
                ag_copy(d, s, k).wait_send()
        return carry

    lax.fori_loop(0, n - 1, drain, 0)


def ring_allreduce(x, n, cid):
    _, _, m, rows, cols = x.shape
    return pl.pallas_call(
        functools.partial(ring_kernel, n, m),
        out_shape=jax.ShapeDtypeStruct(x.shape, x.dtype),
        in_specs=[pl.BlockSpec(memory_space=pltpu.VMEM)],
        out_specs=pl.BlockSpec(memory_space=pltpu.VMEM),
        scratch_shapes=[
            pltpu.VMEM((2, n - 1, m, rows, cols), x.dtype),
            pltpu.SemaphoreType.DMA((2, n - 1, m)),
            pltpu.SemaphoreType.DMA((2, n - 1, m)),
            pltpu.SemaphoreType.DMA((2, n - 1, m)),
            pltpu.SemaphoreType.DMA((2, n - 1, m)),
            pltpu.SemaphoreType.REGULAR,
        ],
        compiler_params=pltpu.CompilerParams(collective_id=cid, has_side_effects=True),
    )(x)


def slot_allreduce(slots, n, cid):
    steps, rows, cols = slots.shape
    total = steps * rows
    sub = 16 if slots.dtype == jnp.bfloat16 else 8
    m = total // (2 * n * sub)
    out = ring_allreduce(slots.reshape(2, n, m, sub, cols), n, cid)
    return out.reshape(steps, rows, cols)


def pair_terms(query_rows, grad_rows, norm_rows, dot_rows, key_rows, value_rows, allowed):
    rows = query_rows.shape[0]
    cols = key_rows.shape[0]
    group = HQ // HK
    scale = 1.0 / math.sqrt(DH)
    query_heads = query_rows.reshape(rows, HK, group, DH)
    grad_heads = grad_rows.reshape(rows, HK, group, DH)
    key_heads = key_rows.reshape(cols, HK, DH)
    value_heads = value_rows.reshape(cols, HK, DH)
    scores = (
        jnp.einsum("qhgd,khd->hgqk", query_heads, key_heads, preferred_element_type=jnp.float32)
        * scale
    )
    norms = norm_rows.reshape(HK, group, rows, 1)
    dots = dot_rows.reshape(HK, group, rows, 1)
    probs = jnp.where(allowed, jnp.exp(scores - norms), jnp.float32(0.0))
    grad_probs = jnp.einsum(
        "qhgd,khd->hgqk", grad_heads, value_heads, preferred_element_type=jnp.float32
    )
    grad_scores = (probs * (grad_probs - dots)).astype(jnp.bfloat16)
    probs_low = probs.astype(jnp.bfloat16)
    grad_q = (
        jnp.einsum(
            "hgqk,khd->qhgd", grad_scores, key_heads, preferred_element_type=jnp.float32
        ).reshape(rows, HQ * DH)
        * scale
    )
    grad_k = (
        jnp.einsum(
            "hgqk,qhgd->khd", grad_scores, query_heads, preferred_element_type=jnp.float32
        ).reshape(cols, HK * DH)
        * scale
    )
    grad_v = jnp.einsum(
        "hgqk,qhgd->khd", probs_low, grad_heads, preferred_element_type=jnp.float32
    ).reshape(cols, HK * DH)
    return (grad_q, grad_k, grad_v)


def allowed_rows(local_routes, query_start, key_start, tokens, widen, active):
    per_dev = local_routes.shape[0]
    query_blocks = query_start // BLK + jnp.arange(per_dev, dtype=jnp.int32)
    key_blocks = key_start // BLK + jnp.arange(per_dev, dtype=jnp.int32)
    listed = jnp.any(local_routes[:, :, None] == key_blocks[None, None, :], axis=1)
    same = query_blocks[:, None] == key_blocks[None, :]
    chosen = listed & (same | widen) & active
    token_level = jnp.broadcast_to(chosen[:, None, :, None], (per_dev, BLK, per_dev, BLK)).reshape(
        tokens, tokens
    )
    positions = jnp.arange(tokens, dtype=jnp.int32)
    causal = key_start + positions[None, :] <= query_start + positions[:, None]
    return token_level & causal


def make_on_device(n):
    def on_device(
        queries, key_states, value_states, grad_output, log_norms, grad_dots, block_routes, owner_steps
    ):
        tokens = queries.shape[0]
        features = key_states.shape[1]
        device = lax.axis_index("ctx")
        start = device * tokens
        steps = owner_steps.shape[0]
        is_mine = owner_steps == device
        covered = jnp.any(is_mine)
        kv = jnp.concatenate([key_states, value_states], axis=1)
        kv_slots = jnp.where(is_mine[:, None, None], kv[None], jnp.zeros((), kv.dtype))
        kv_all = slot_allreduce(kv_slots, n, 0)
        local_mask = allowed_rows(block_routes, start, start, tokens, covered, jnp.ones((), jnp.bool_))
        grad_q, grad_k, grad_v = pair_terms(
            queries, grad_output, log_norms, grad_dots, key_states, value_states, local_mask
        )
        terms = []
        for step in range(steps):
            owner = owner_steps[step]
            key_part = kv_all[step, :, :features]
            value_part = kv_all[step, :, features:]
            step_mask = allowed_rows(
                block_routes, start, owner * tokens, tokens, jnp.ones((), jnp.bool_), owner != device
            )
            term_q, term_k, term_v = pair_terms(
                queries, grad_output, log_norms, grad_dots, key_part, value_part, step_mask
            )
            grad_q = grad_q + term_q
            terms.append(jnp.concatenate([term_k, term_v], axis=1))
        summed = slot_allreduce(jnp.stack(terms), n, 1)
        for step in range(steps):
            taken = is_mine[step]
            grad_k = grad_k + jnp.where(taken, summed[step, :, :features], jnp.float32(0.0))
            grad_v = grad_v + jnp.where(taken, summed[step, :, features:], jnp.float32(0.0))
        return (grad_q.astype(jnp.bfloat16), grad_k.astype(jnp.bfloat16), grad_v.astype(jnp.bfloat16))

    return on_device


def solution(mesh):
    n = mesh.shape["ctx"]
    return jax.shard_map(
        make_on_device(n),
        mesh=mesh,
        in_specs=(
            P(("dp", "ctx"), None),
            P(("dp", "ctx"), None),
            P(("dp", "ctx"), None),
            P(("dp", "ctx"), None),
            P(None, ("dp", "ctx")),
            P(None, ("dp", "ctx")),
            P(("dp", "ctx"), None),
            P("dp"),
        ),
        out_specs=(P(("dp", "ctx"), None), P(("dp", "ctx"), None), P(("dp", "ctx"), None)),
        check_vma=False,
    )
```

```python
import functools
import math

import jax
import jax.numpy as jnp
from jax import lax
from jax.experimental import pallas as pl
from jax.experimental.pallas import tpu as pltpu
from jax.sharding import PartitionSpec as P

HQ = 16
HK = 4
DH = 128
BLK = 256
MESH = pl.DeviceIdType.MESH


def grid_kernel(nz, m, x_ref, o_ref, rbuf, ybuf, rs_send, rs_recv, y_send, y_recv, ag_send,
                ag_recv, ready):
    me = lax.axis_index("ctx")
    row = lax.axis_index("dp")
    z = me // 2
    y = me % 2
    right = ((z + 1) % nz) * 2 + y
    left = ((z + nz - 1) % nz) * 2 + y
    partner = z * 2 + (1 - y)
    peers = (right, left)

    barrier = pltpu.get_barrier_semaphore()
    for nb in (left, right, partner):
        pl.semaphore_signal(barrier, inc=1, device_id=(row, nb), device_id_type=MESH)
    pl.semaphore_wait(barrier, 3)

    o_ref[...] = x_ref[...]

    def rs_copy(d, s, k):
        send = (z + nz - s) % nz if d == 0 else (z + s) % nz
        return pltpu.make_async_remote_copy(
            src_ref=o_ref.at[d, send, k],
            dst_ref=rbuf.at[d, s, k],
            send_sem=rs_send.at[d, s, k],
            recv_sem=rs_recv.at[d, s, k],
            device_id=(row, peers[d]),
            device_id_type=MESH,
        )

    for k in range(m):
        for d in range(2):
            rs_copy(d, 0, k).start()

    def rs_step(s, carry):
        for k in range(m):
            for d in range(2):
                rs_copy(d, s, k).wait_recv()
                got = (z + 2 * nz - s - 1) % nz if d == 0 else (z + s + 1) % nz
                o_ref[d, got, k] = o_ref[d, got, k] + rbuf[d, s, k]

                @pl.when(s < nz - 2)
                def _():
                    rs_copy(d, s + 1, k).start()

        return carry

    lax.fori_loop(0, nz - 1, rs_step, 0)

    mine = ((z + 1) % nz, (z + nz - 1) % nz)

    def y_copy(d, k):
        return pltpu.make_async_remote_copy(
            src_ref=o_ref.at[d, mine[d], k],
            dst_ref=ybuf.at[d, k],
            send_sem=y_send.at[d, k],
            recv_sem=y_recv.at[d, k],
            device_id=(row, partner),
            device_id_type=MESH,
        )

    for k in range(m):
        for d in range(2):
            y_copy(d, k).start()
    for k in range(m):
        for d in range(2):
            c = y_copy(d, k)
            c.wait_recv()
            c.wait_send()
            o_ref[d, mine[d], k] = o_ref[d, mine[d], k] + ybuf[d, k]

    def rs_drain(s, carry):
        for k in range(m):
            for d in range(2):
                rs_copy(d, s, k).wait_send()
        return carry

    lax.fori_loop(0, nz - 1, rs_drain, 0)
    for nb in (left, right):
        pl.semaphore_signal(ready, inc=1, device_id=(row, nb), device_id_type=MESH)
    pl.semaphore_wait(ready, 2)

    def ag_copy(d, t, k):
        chunk = (z + 1 + nz - t) % nz if d == 0 else (z + nz - 1 + t) % nz
        return pltpu.make_async_remote_copy(
            src_ref=o_ref.at[d, chunk, k],
            dst_ref=o_ref.at[d, chunk, k],
            send_sem=ag_send.at[d, t, k],
            recv_sem=ag_recv.at[d, t, k],
            device_id=(row, peers[d]),
            device_id_type=MESH,
        )

    for k in range(m):
        for d in range(2):
            ag_copy(d, 0, k).start()

    def ag_step(t, carry):
        for k in range(m):
            for d in range(2):
                ag_copy(d, t, k).wait_recv()

                @pl.when(t < nz - 2)
                def _():
                    ag_copy(d, t + 1, k).start()

        return carry

    lax.fori_loop(0, nz - 1, ag_step, 0)

    def drain(s, carry):
        for k in range(m):
            for d in range(2):
                ag_copy(d, s, k).wait_send()
        return carry

    lax.fori_loop(0, nz - 1, drain, 0)


def grid_allreduce(x, cid):
    _, nz, m, rows, cols = x.shape
    return pl.pallas_call(
        functools.partial(grid_kernel, nz, m),
        out_shape=jax.ShapeDtypeStruct(x.shape, x.dtype),
        in_specs=[pl.BlockSpec(memory_space=pltpu.VMEM)],
        out_specs=pl.BlockSpec(memory_space=pltpu.VMEM),
        scratch_shapes=[
            pltpu.VMEM((2, nz - 1, m, rows, cols), x.dtype),
            pltpu.VMEM((2, m, rows, cols), x.dtype),
            pltpu.SemaphoreType.DMA((2, nz - 1, m)),
            pltpu.SemaphoreType.DMA((2, nz - 1, m)),
            pltpu.SemaphoreType.DMA((2, m)),
            pltpu.SemaphoreType.DMA((2, m)),
            pltpu.SemaphoreType.DMA((2, nz - 1, m)),
            pltpu.SemaphoreType.DMA((2, nz - 1, m)),
            pltpu.SemaphoreType.REGULAR,
        ],
        compiler_params=pltpu.CompilerParams(collective_id=cid, has_side_effects=True),
    )(x)


def slot_allreduce(slots, n, cid):
    steps, rows, cols = slots.shape
    total = steps * rows
    sub = 16 if slots.dtype == jnp.bfloat16 else 8
    nz = n // 2
    m = total // (2 * nz * sub)
    out = grid_allreduce(slots.reshape(2, nz, m, sub, cols), cid)
    return out.reshape(steps, rows, cols)


def pair_terms(query_rows, grad_rows, norm_rows, dot_rows, key_rows, value_rows, allowed):
    rows = query_rows.shape[0]
    cols = key_rows.shape[0]
    group = HQ // HK
    scale = 1.0 / math.sqrt(DH)
    query_heads = query_rows.reshape(rows, HK, group, DH)
    grad_heads = grad_rows.reshape(rows, HK, group, DH)
    key_heads = key_rows.reshape(cols, HK, DH)
    value_heads = value_rows.reshape(cols, HK, DH)
    scores = (
        jnp.einsum("qhgd,khd->hgqk", query_heads, key_heads, preferred_element_type=jnp.float32)
        * scale
    )
    norms = norm_rows.reshape(HK, group, rows, 1)
    dots = dot_rows.reshape(HK, group, rows, 1)
    probs = jnp.where(allowed, jnp.exp(scores - norms), jnp.float32(0.0))
    grad_probs = jnp.einsum(
        "qhgd,khd->hgqk", grad_heads, value_heads, preferred_element_type=jnp.float32
    )
    grad_scores = (probs * (grad_probs - dots)).astype(jnp.bfloat16)
    probs_low = probs.astype(jnp.bfloat16)
    grad_q = (
        jnp.einsum(
            "hgqk,khd->qhgd", grad_scores, key_heads, preferred_element_type=jnp.float32
        ).reshape(rows, HQ * DH)
        * scale
    )
    grad_k = (
        jnp.einsum(
            "hgqk,qhgd->khd", grad_scores, query_heads, preferred_element_type=jnp.float32
        ).reshape(cols, HK * DH)
        * scale
    )
    grad_v = jnp.einsum(
        "hgqk,qhgd->khd", probs_low, grad_heads, preferred_element_type=jnp.float32
    ).reshape(cols, HK * DH)
    return (grad_q, grad_k, grad_v)


def allowed_rows(local_routes, query_start, key_start, tokens, widen, active):
    per_dev = local_routes.shape[0]
    query_blocks = query_start // BLK + jnp.arange(per_dev, dtype=jnp.int32)
    key_blocks = key_start // BLK + jnp.arange(per_dev, dtype=jnp.int32)
    listed = jnp.any(local_routes[:, :, None] == key_blocks[None, None, :], axis=1)
    same = query_blocks[:, None] == key_blocks[None, :]
    chosen = listed & (same | widen) & active
    token_level = jnp.broadcast_to(chosen[:, None, :, None], (per_dev, BLK, per_dev, BLK)).reshape(
        tokens, tokens
    )
    positions = jnp.arange(tokens, dtype=jnp.int32)
    causal = key_start + positions[None, :] <= query_start + positions[:, None]
    return token_level & causal


def make_on_device(n):
    def on_device(
        queries, key_states, value_states, grad_output, log_norms, grad_dots, block_routes, owner_steps
    ):
        tokens = queries.shape[0]
        features = key_states.shape[1]
        device = lax.axis_index("ctx")
        start = device * tokens
        steps = owner_steps.shape[0]
        is_mine = owner_steps == device
        covered = jnp.any(is_mine)
        kv = jnp.concatenate([key_states, value_states], axis=1)
        kv_slots = jnp.where(is_mine[:, None, None], kv[None], jnp.zeros((), kv.dtype))
        kv_all = slot_allreduce(kv_slots, n, 0)
        local_mask = allowed_rows(block_routes, start, start, tokens, covered, jnp.ones((), jnp.bool_))
        grad_q, grad_k, grad_v = pair_terms(
            queries, grad_output, log_norms, grad_dots, key_states, value_states, local_mask
        )
        terms = []
        for step in range(steps):
            owner = owner_steps[step]
            key_part = kv_all[step, :, :features]
            value_part = kv_all[step, :, features:]
            step_mask = allowed_rows(
                block_routes, start, owner * tokens, tokens, jnp.ones((), jnp.bool_), owner != device
            )
            term_q, term_k, term_v = pair_terms(
                queries, grad_output, log_norms, grad_dots, key_part, value_part, step_mask
            )
            grad_q = grad_q + term_q
            terms.append(jnp.concatenate([term_k, term_v], axis=1))
        summed = slot_allreduce(jnp.stack(terms), n, 1)
        for step in range(steps):
            taken = is_mine[step]
            grad_k = grad_k + jnp.where(taken, summed[step, :, :features], jnp.float32(0.0))
            grad_v = grad_v + jnp.where(taken, summed[step, :, features:], jnp.float32(0.0))
        return (grad_q.astype(jnp.bfloat16), grad_k.astype(jnp.bfloat16), grad_v.astype(jnp.bfloat16))

    return on_device


def solution(mesh):
    n = mesh.shape["ctx"]
    return jax.shard_map(
        make_on_device(n),
        mesh=mesh,
        in_specs=(
            P(("dp", "ctx"), None),
            P(("dp", "ctx"), None),
            P(("dp", "ctx"), None),
            P(("dp", "ctx"), None),
            P(None, ("dp", "ctx")),
            P(None, ("dp", "ctx")),
            P(("dp", "ctx"), None),
            P("dp"),
        ),
        out_specs=(P(("dp", "ctx"), None), P(("dp", "ctx"), None), P(("dp", "ctx"), None)),
        check_vma=False,
    )
```

```python
import functools
import math

import jax
import jax.numpy as jnp
from jax import lax
from jax.experimental import pallas as pl
from jax.experimental.pallas import tpu as pltpu
from jax.sharding import PartitionSpec as P

HQ = 16
HK = 4
DH = 128
BLK = 256
MESH = pl.DeviceIdType.MESH


def grid_kernel(nz, m, x_ref, o_ref, rbuf, ybuf, rs_send, rs_recv, y_send, y_recv, ag_send,
                ag_recv, ready):
    me = lax.axis_index("ctx")
    row = lax.axis_index("dp")
    z = me // 2
    y = me % 2
    right = ((z + 1) % nz) * 2 + y
    left = ((z + nz - 1) % nz) * 2 + y
    partner = z * 2 + (1 - y)
    peers = (right, left)

    barrier = pltpu.get_barrier_semaphore()
    for nb in (left, right, partner):
        pl.semaphore_signal(barrier, inc=1, device_id=(row, nb), device_id_type=MESH)
    pl.semaphore_wait(barrier, 3)

    o_ref[...] = x_ref[...]

    def rs_copy(d, s, k):
        send = (z + nz - s) % nz if d == 0 else (z + s) % nz
        return pltpu.make_async_remote_copy(
            src_ref=o_ref.at[d, send, k],
            dst_ref=rbuf.at[d, s, k],
            send_sem=rs_send.at[d, s, k],
            recv_sem=rs_recv.at[d, s, k],
            device_id=(row, peers[d]),
            device_id_type=MESH,
        )

    for k in range(m):
        for d in range(2):
            rs_copy(d, 0, k).start()

    def rs_step(s, carry):
        for k in range(m):
            for d in range(2):
                rs_copy(d, s, k).wait_recv()
                got = (z + 2 * nz - s - 1) % nz if d == 0 else (z + s + 1) % nz
                o_ref[d, got, k] = o_ref[d, got, k] + rbuf[d, s, k]

                @pl.when(s < nz - 2)
                def _():
                    rs_copy(d, s + 1, k).start()

        return carry

    lax.fori_loop(0, nz - 1, rs_step, 0)

    mine = ((z + 1) % nz, (z + nz - 1) % nz)

    def y_copy(d, k):
        return pltpu.make_async_remote_copy(
            src_ref=o_ref.at[d, mine[d], k],
            dst_ref=ybuf.at[d, k],
            send_sem=y_send.at[d, k],
            recv_sem=y_recv.at[d, k],
            device_id=(row, partner),
            device_id_type=MESH,
        )

    for k in range(m):
        for d in range(2):
            y_copy(d, k).start()
    for k in range(m):
        for d in range(2):
            c = y_copy(d, k)
            c.wait_recv()
            c.wait_send()
            o_ref[d, mine[d], k] = o_ref[d, mine[d], k] + ybuf[d, k]

    def rs_drain(s, carry):
        for k in range(m):
            for d in range(2):
                rs_copy(d, s, k).wait_send()
        return carry

    lax.fori_loop(0, nz - 1, rs_drain, 0)
    for nb in (left, right):
        pl.semaphore_signal(ready, inc=1, device_id=(row, nb), device_id_type=MESH)
    pl.semaphore_wait(ready, 2)

    def ag_copy(d, t, k):
        chunk = (z + 1 + nz - t) % nz if d == 0 else (z + nz - 1 + t) % nz
        return pltpu.make_async_remote_copy(
            src_ref=o_ref.at[d, chunk, k],
            dst_ref=o_ref.at[d, chunk, k],
            send_sem=ag_send.at[d, t, k],
            recv_sem=ag_recv.at[d, t, k],
            device_id=(row, peers[d]),
            device_id_type=MESH,
        )

    for k in range(m):
        for d in range(2):
            ag_copy(d, 0, k).start()

    def ag_step(t, carry):
        for k in range(m):
            for d in range(2):
                ag_copy(d, t, k).wait_recv()

                @pl.when(t < nz - 2)
                def _():
                    ag_copy(d, t + 1, k).start()

        return carry

    lax.fori_loop(0, nz - 1, ag_step, 0)

    def drain(s, carry):
        for k in range(m):
            for d in range(2):
                ag_copy(d, s, k).wait_send()
        return carry

    lax.fori_loop(0, nz - 1, drain, 0)


def grid_allreduce(x, cid):
    _, nz, m, rows, cols = x.shape
    return pl.pallas_call(
        functools.partial(grid_kernel, nz, m),
        out_shape=jax.ShapeDtypeStruct(x.shape, x.dtype),
        in_specs=[pl.BlockSpec(memory_space=pltpu.VMEM)],
        out_specs=pl.BlockSpec(memory_space=pltpu.VMEM),
        scratch_shapes=[
            pltpu.VMEM((2, nz - 1, m, rows, cols), x.dtype),
            pltpu.VMEM((2, m, rows, cols), x.dtype),
            pltpu.SemaphoreType.DMA((2, nz - 1, m)),
            pltpu.SemaphoreType.DMA((2, nz - 1, m)),
            pltpu.SemaphoreType.DMA((2, m)),
            pltpu.SemaphoreType.DMA((2, m)),
            pltpu.SemaphoreType.DMA((2, nz - 1, m)),
            pltpu.SemaphoreType.DMA((2, nz - 1, m)),
            pltpu.SemaphoreType.REGULAR,
        ],
        compiler_params=pltpu.CompilerParams(collective_id=cid, has_side_effects=True),
    )(x)


def slot_allreduce(slots, n, cid):
    steps, rows, cols = slots.shape
    total = steps * rows
    sub = 16 if slots.dtype == jnp.bfloat16 else 8
    nz = n // 2
    m = total // (2 * nz * sub)
    out = grid_allreduce(slots.reshape(2, nz, m, sub, cols), cid)
    return out.reshape(steps, rows, cols)


def pair_terms(query_rows, grad_rows, norm_rows, dot_rows, key_rows, value_rows, allowed):
    rows = query_rows.shape[0]
    cols = key_rows.shape[0]
    group = HQ // HK
    scale = 1.0 / math.sqrt(DH)
    query_heads = query_rows.reshape(rows, HK, group, DH)
    grad_heads = grad_rows.reshape(rows, HK, group, DH)
    key_heads = key_rows.reshape(cols, HK, DH)
    value_heads = value_rows.reshape(cols, HK, DH)
    scores = (
        jnp.einsum("qhgd,khd->hgqk", query_heads, key_heads, preferred_element_type=jnp.float32)
        * scale
    )
    norms = norm_rows.reshape(HK, group, rows, 1)
    dots = dot_rows.reshape(HK, group, rows, 1)
    probs = jnp.where(allowed, jnp.exp(scores - norms), jnp.float32(0.0))
    grad_probs = jnp.einsum(
        "qhgd,khd->hgqk", grad_heads, value_heads, preferred_element_type=jnp.float32
    )
    grad_scores = (probs * (grad_probs - dots)).astype(jnp.bfloat16)
    probs_low = probs.astype(jnp.bfloat16)
    grad_q = (
        jnp.einsum(
            "hgqk,khd->qhgd", grad_scores, key_heads, preferred_element_type=jnp.float32
        ).reshape(rows, HQ * DH)
        * scale
    )
    grad_k = (
        jnp.einsum(
            "hgqk,qhgd->khd", grad_scores, query_heads, preferred_element_type=jnp.float32
        ).reshape(cols, HK * DH)
        * scale
    )
    grad_v = jnp.einsum(
        "hgqk,qhgd->khd", probs_low, grad_heads, preferred_element_type=jnp.float32
    ).reshape(cols, HK * DH)
    return (grad_q, grad_k, grad_v)


def allowed_rows(local_routes, query_start, key_start, tokens, widen, active):
    per_dev = local_routes.shape[0]
    query_blocks = query_start // BLK + jnp.arange(per_dev, dtype=jnp.int32)
    key_blocks = key_start // BLK + jnp.arange(per_dev, dtype=jnp.int32)
    listed = jnp.any(local_routes[:, :, None] == key_blocks[None, None, :], axis=1)
    same = query_blocks[:, None] == key_blocks[None, :]
    chosen = listed & (same | widen) & active
    token_level = jnp.broadcast_to(chosen[:, None, :, None], (per_dev, BLK, per_dev, BLK)).reshape(
        tokens, tokens
    )
    positions = jnp.arange(tokens, dtype=jnp.int32)
    causal = key_start + positions[None, :] <= query_start + positions[:, None]
    return token_level & causal


def make_on_device(n):
    def on_device(
        queries, key_states, value_states, grad_output, log_norms, grad_dots, block_routes, owner_steps
    ):
        tokens = queries.shape[0]
        features = key_states.shape[1]
        device = lax.axis_index("ctx")
        start = device * tokens
        steps = owner_steps.shape[0]
        is_mine = owner_steps == device
        covered = jnp.any(is_mine)
        kv = jnp.concatenate([key_states, value_states], axis=1)
        kv_slots = jnp.where(is_mine[:, None, None], kv[None], jnp.zeros((), kv.dtype))
        kv_all = slot_allreduce(kv_slots, n, 0)
        local_mask = allowed_rows(block_routes, start, start, tokens, covered, jnp.ones((), jnp.bool_))
        masks = [local_mask]
        for step in range(steps):
            owner = owner_steps[step]
            masks.append(
                allowed_rows(
                    block_routes, start, owner * tokens, tokens, jnp.ones((), jnp.bool_), owner != device
                )
            )
        key_cols = jnp.concatenate(
            [key_states, kv_all[:, :, :features].reshape(steps * tokens, features)], axis=0
        )
        value_cols = jnp.concatenate(
            [value_states, kv_all[:, :, features:].reshape(steps * tokens, features)], axis=0
        )
        grad_q, grad_k_all, grad_v_all = pair_terms(
            queries, grad_output, log_norms, grad_dots, key_cols, value_cols,
            jnp.concatenate(masks, axis=1),
        )
        grad_k = grad_k_all[:tokens]
        grad_v = grad_v_all[:tokens]
        terms = jnp.concatenate(
            [
                grad_k_all[tokens:].reshape(steps, tokens, features),
                grad_v_all[tokens:].reshape(steps, tokens, features),
            ],
            axis=2,
        )
        summed = slot_allreduce(terms, n, 1)
        for step in range(steps):
            taken = is_mine[step]
            grad_k = grad_k + jnp.where(taken, summed[step, :, :features], jnp.float32(0.0))
            grad_v = grad_v + jnp.where(taken, summed[step, :, features:], jnp.float32(0.0))
        return (grad_q.astype(jnp.bfloat16), grad_k.astype(jnp.bfloat16), grad_v.astype(jnp.bfloat16))

    return on_device


def solution(mesh):
    n = mesh.shape["ctx"]
    return jax.shard_map(
        make_on_device(n),
        mesh=mesh,
        in_specs=(
            P(("dp", "ctx"), None),
            P(("dp", "ctx"), None),
            P(("dp", "ctx"), None),
            P(("dp", "ctx"), None),
            P(None, ("dp", "ctx")),
            P(None, ("dp", "ctx")),
            P(("dp", "ctx"), None),
            P("dp"),
        ),
        out_specs=(P(("dp", "ctx"), None), P(("dp", "ctx"), None), P(("dp", "ctx"), None)),
        check_vma=False,
    )
```

```python
import functools
import math

import jax
import jax.numpy as jnp
from jax import lax
from jax.experimental import pallas as pl
from jax.experimental.pallas import tpu as pltpu
from jax.sharding import PartitionSpec as P

HQ = 16
HK = 4
DH = 128
BLK = 256
MESH = pl.DeviceIdType.MESH


def grid_kernel(nz, m, x_ref, o_ref, rbuf, ybuf, rs_send, rs_recv, y_send, y_recv, ag_send,
                ag_recv, ready):
    me = lax.axis_index("ctx")
    row = lax.axis_index("dp")
    z = me // 2
    y = me % 2
    right = ((z + 1) % nz) * 2 + y
    left = ((z + nz - 1) % nz) * 2 + y
    partner = z * 2 + (1 - y)
    peers = (right, left)

    barrier = pltpu.get_barrier_semaphore()
    for nb in (left, right, partner):
        pl.semaphore_signal(barrier, inc=1, device_id=(row, nb), device_id_type=MESH)
    pl.semaphore_wait(barrier, 3)

    o_ref[...] = x_ref[...]

    def rs_copy(d, s, k):
        send = (z + nz - s) % nz if d == 0 else (z + s) % nz
        return pltpu.make_async_remote_copy(
            src_ref=o_ref.at[d, send, k],
            dst_ref=rbuf.at[d, s, k],
            send_sem=rs_send.at[d, s, k],
            recv_sem=rs_recv.at[d, s, k],
            device_id=(row, peers[d]),
            device_id_type=MESH,
        )

    for k in range(m):
        for d in range(2):
            rs_copy(d, 0, k).start()

    def rs_step(s, carry):
        for k in range(m):
            for d in range(2):
                rs_copy(d, s, k).wait_recv()
                got = (z + 2 * nz - s - 1) % nz if d == 0 else (z + s + 1) % nz
                o_ref[d, got, k] = o_ref[d, got, k] + rbuf[d, s, k]

                @pl.when(s < nz - 2)
                def _():
                    rs_copy(d, s + 1, k).start()

        return carry

    lax.fori_loop(0, nz - 1, rs_step, 0)

    mine = ((z + 1) % nz, (z + nz - 1) % nz)

    def y_copy(d, k):
        return pltpu.make_async_remote_copy(
            src_ref=o_ref.at[d, mine[d], k],
            dst_ref=ybuf.at[d, k],
            send_sem=y_send.at[d, k],
            recv_sem=y_recv.at[d, k],
            device_id=(row, partner),
            device_id_type=MESH,
        )

    for k in range(m):
        for d in range(2):
            y_copy(d, k).start()
    for k in range(m):
        for d in range(2):
            c = y_copy(d, k)
            c.wait_recv()
            c.wait_send()
            o_ref[d, mine[d], k] = o_ref[d, mine[d], k] + ybuf[d, k]

    def rs_drain(s, carry):
        for k in range(m):
            for d in range(2):
                rs_copy(d, s, k).wait_send()
        return carry

    lax.fori_loop(0, nz - 1, rs_drain, 0)
    for nb in (left, right):
        pl.semaphore_signal(ready, inc=1, device_id=(row, nb), device_id_type=MESH)
    pl.semaphore_wait(ready, 2)

    def ag_copy(d, t, k):
        chunk = (z + 1 + nz - t) % nz if d == 0 else (z + nz - 1 + t) % nz
        return pltpu.make_async_remote_copy(
            src_ref=o_ref.at[d, chunk, k],
            dst_ref=o_ref.at[d, chunk, k],
            send_sem=ag_send.at[d, t, k],
            recv_sem=ag_recv.at[d, t, k],
            device_id=(row, peers[d]),
            device_id_type=MESH,
        )

    for k in range(m):
        for d in range(2):
            ag_copy(d, 0, k).start()

    def ag_step(t, carry):
        for k in range(m):
            for d in range(2):
                ag_copy(d, t, k).wait_recv()

                @pl.when(t < nz - 2)
                def _():
                    ag_copy(d, t + 1, k).start()

        return carry

    lax.fori_loop(0, nz - 1, ag_step, 0)

    def drain(s, carry):
        for k in range(m):
            for d in range(2):
                ag_copy(d, s, k).wait_send()
        return carry

    lax.fori_loop(0, nz - 1, drain, 0)


def grid_allreduce(x, cid):
    _, nz, m, rows, cols = x.shape
    return pl.pallas_call(
        functools.partial(grid_kernel, nz, m),
        out_shape=jax.ShapeDtypeStruct(x.shape, x.dtype),
        in_specs=[pl.BlockSpec(memory_space=pltpu.VMEM)],
        out_specs=pl.BlockSpec(memory_space=pltpu.VMEM),
        scratch_shapes=[
            pltpu.VMEM((2, nz - 1, m, rows, cols), x.dtype),
            pltpu.VMEM((2, m, rows, cols), x.dtype),
            pltpu.SemaphoreType.DMA((2, nz - 1, m)),
            pltpu.SemaphoreType.DMA((2, nz - 1, m)),
            pltpu.SemaphoreType.DMA((2, m)),
            pltpu.SemaphoreType.DMA((2, m)),
            pltpu.SemaphoreType.DMA((2, nz - 1, m)),
            pltpu.SemaphoreType.DMA((2, nz - 1, m)),
            pltpu.SemaphoreType.REGULAR,
        ],
        compiler_params=pltpu.CompilerParams(collective_id=cid, has_side_effects=True),
    )(x)


def slot_allreduce(slots, n, cid):
    steps, rows, cols = slots.shape
    total = steps * rows
    sub = 16 if slots.dtype == jnp.bfloat16 else 8
    nz = n // 2
    m = total // (2 * nz * sub)
    out = grid_allreduce(slots.reshape(2, nz, m, sub, cols), cid)
    return out.reshape(steps, rows, cols)


def pair_kernel(scale, group, q_ref, do_ref, k_ref, v_ref, lse_ref, dot_ref, mask_ref, dq_ref,
                dk_ref, dv_ref):
    h = pl.program_id(0)
    qh = q_ref[...]
    doh = do_ref[...]
    kg = k_ref[...]
    vg = v_ref[...]
    nt = (((1,), (1,)), ((), ()))
    scores = lax.dot_general(kg, qh, nt, preferred_element_type=jnp.float32) * scale
    lse = lse_ref[pl.ds(h, 1), :]
    dots = dot_ref[pl.ds(h, 1), :]
    probs = jnp.where(mask_ref[...] > 0, jnp.exp(scores - lse), jnp.float32(0.0))
    grad_probs = lax.dot_general(vg, doh, nt, preferred_element_type=jnp.float32)
    grad_scores = (probs * (grad_probs - dots)).astype(jnp.bfloat16)
    probs_low = probs.astype(jnp.bfloat16)
    tn = (((0,), (0,)), ((), ()))
    dq = lax.dot_general(grad_scores, kg, tn, preferred_element_type=jnp.float32) * scale
    dq_ref[...] = dq.astype(dq_ref.dtype)
    dk = jnp.dot(grad_scores, qh, preferred_element_type=jnp.float32) * scale
    dv = jnp.dot(probs_low, doh, preferred_element_type=jnp.float32)

    @pl.when(h % group == 0)
    def _():
        dk_ref[...] = dk
        dv_ref[...] = dv

    @pl.when(h % group != 0)
    def _():
        dk_ref[...] += dk
        dv_ref[...] += dv


def pair_terms(query_rows, grad_rows, norm_rows, dot_rows, key_rows, value_rows, allowed):
    rows = query_rows.shape[0]
    cols = key_rows.shape[0]
    group = HQ // HK
    scale = 1.0 / math.sqrt(DH)
    return pl.pallas_call(
        functools.partial(pair_kernel, scale, group),
        out_shape=(
            jax.ShapeDtypeStruct((rows, HQ * DH), jnp.bfloat16),
            jax.ShapeDtypeStruct((cols, HK * DH), jnp.float32),
            jax.ShapeDtypeStruct((cols, HK * DH), jnp.float32),
        ),
        grid=(HQ,),
        in_specs=[
            pl.BlockSpec((rows, DH), lambda h: (0, h)),
            pl.BlockSpec((rows, DH), lambda h: (0, h)),
            pl.BlockSpec((cols, DH), lambda h: (0, h // group)),
            pl.BlockSpec((cols, DH), lambda h: (0, h // group)),
            pl.BlockSpec((HQ, rows), lambda h: (0, 0)),
            pl.BlockSpec((HQ, rows), lambda h: (0, 0)),
            pl.BlockSpec((cols, rows), lambda h: (0, 0)),
        ],
        out_specs=[
            pl.BlockSpec((rows, DH), lambda h: (0, h)),
            pl.BlockSpec((cols, DH), lambda h: (0, h // group)),
            pl.BlockSpec((cols, DH), lambda h: (0, h // group)),
        ],
        compiler_params=pltpu.CompilerParams(dimension_semantics=("arbitrary",)),
    )(query_rows, grad_rows, key_rows, value_rows, norm_rows, dot_rows, allowed)


def allowed_rows(local_routes, query_start, key_start, tokens, widen, active):
    per_dev = local_routes.shape[0]
    query_blocks = query_start // BLK + jnp.arange(per_dev, dtype=jnp.int32)
    key_blocks = key_start // BLK + jnp.arange(per_dev, dtype=jnp.int32)
    listed = jnp.any(local_routes[:, :, None] == key_blocks[None, None, :], axis=1)
    same = query_blocks[:, None] == key_blocks[None, :]
    chosen = listed & (same | widen) & active
    token_level = jnp.broadcast_to(chosen[:, None, :, None], (per_dev, BLK, per_dev, BLK)).reshape(
        tokens, tokens
    )
    positions = jnp.arange(tokens, dtype=jnp.int32)
    causal = key_start + positions[None, :] <= query_start + positions[:, None]
    return token_level & causal


def make_on_device(n):
    def on_device(
        queries, key_states, value_states, grad_output, log_norms, grad_dots, block_routes, owner_steps
    ):
        tokens = queries.shape[0]
        features = key_states.shape[1]
        device = lax.axis_index("ctx")
        start = device * tokens
        steps = owner_steps.shape[0]
        is_mine = owner_steps == device
        covered = jnp.any(is_mine)
        kv = jnp.concatenate([key_states, value_states], axis=1)
        kv_slots = jnp.where(is_mine[:, None, None], kv[None], jnp.zeros((), kv.dtype))
        kv_all = slot_allreduce(kv_slots, n, 0)
        local_mask = allowed_rows(block_routes, start, start, tokens, covered, jnp.ones((), jnp.bool_))
        masks = [local_mask]
        for step in range(steps):
            owner = owner_steps[step]
            masks.append(
                allowed_rows(
                    block_routes, start, owner * tokens, tokens, jnp.ones((), jnp.bool_), owner != device
                )
            )
        key_cols = jnp.concatenate(
            [key_states, kv_all[:, :, :features].reshape(steps * tokens, features)], axis=0
        )
        value_cols = jnp.concatenate(
            [value_states, kv_all[:, :, features:].reshape(steps * tokens, features)], axis=0
        )
        grad_q, grad_k_all, grad_v_all = pair_terms(
            queries, grad_output, log_norms, grad_dots, key_cols, value_cols,
            jnp.concatenate(masks, axis=1).T.astype(jnp.float32),
        )
        grad_k = grad_k_all[:tokens]
        grad_v = grad_v_all[:tokens]
        terms = jnp.concatenate(
            [
                grad_k_all[tokens:].reshape(steps, tokens, features),
                grad_v_all[tokens:].reshape(steps, tokens, features),
            ],
            axis=2,
        )
        summed = slot_allreduce(terms, n, 1)
        for step in range(steps):
            taken = is_mine[step]
            grad_k = grad_k + jnp.where(taken, summed[step, :, :features], jnp.float32(0.0))
            grad_v = grad_v + jnp.where(taken, summed[step, :, features:], jnp.float32(0.0))
        return (grad_q, grad_k.astype(jnp.bfloat16), grad_v.astype(jnp.bfloat16))

    return on_device


def solution(mesh):
    n = mesh.shape["ctx"]
    return jax.shard_map(
        make_on_device(n),
        mesh=mesh,
        in_specs=(
            P(("dp", "ctx"), None),
            P(("dp", "ctx"), None),
            P(("dp", "ctx"), None),
            P(("dp", "ctx"), None),
            P(None, ("dp", "ctx")),
            P(None, ("dp", "ctx")),
            P(("dp", "ctx"), None),
            P("dp"),
        ),
        out_specs=(P(("dp", "ctx"), None), P(("dp", "ctx"), None), P(("dp", "ctx"), None)),
        check_vma=False,
    )
```

```python
import functools
import math

import jax
import jax.numpy as jnp
from jax import lax
from jax.experimental import pallas as pl
from jax.experimental.pallas import tpu as pltpu
from jax.sharding import PartitionSpec as P

HQ = 16
HK = 4
DH = 128
BLK = 256
MESH = pl.DeviceIdType.MESH


def grid_kernel(nz, m, x_ref, o_ref, rbuf, ybuf, rs_send, rs_recv, y_send, y_recv, ag_send,
                ag_recv, ready):
    me = lax.axis_index("ctx")
    row = lax.axis_index("dp")
    z = me // 2
    y = me % 2
    right = ((z + 1) % nz) * 2 + y
    left = ((z + nz - 1) % nz) * 2 + y
    partner = z * 2 + (1 - y)
    peers = (right, left)

    barrier = pltpu.get_barrier_semaphore()
    for nb in (left, right, partner):
        pl.semaphore_signal(barrier, inc=1, device_id=(row, nb), device_id_type=MESH)
    pl.semaphore_wait(barrier, 3)

    o_ref[...] = x_ref[...]

    def rs_copy(d, s, k):
        send = (z + nz - s) % nz if d == 0 else (z + s) % nz
        return pltpu.make_async_remote_copy(
            src_ref=o_ref.at[d, send, k],
            dst_ref=rbuf.at[d, s, k],
            send_sem=rs_send.at[d, s, k],
            recv_sem=rs_recv.at[d, s, k],
            device_id=(row, peers[d]),
            device_id_type=MESH,
        )

    for k in range(m):
        for d in range(2):
            rs_copy(d, 0, k).start()

    def rs_step(s, carry):
        for k in range(m):
            for d in range(2):
                rs_copy(d, s, k).wait_recv()
                got = (z + 2 * nz - s - 1) % nz if d == 0 else (z + s + 1) % nz
                o_ref[d, got, k] = o_ref[d, got, k] + rbuf[d, s, k]

                @pl.when(s < nz - 2)
                def _():
                    rs_copy(d, s + 1, k).start()

        return carry

    lax.fori_loop(0, nz - 1, rs_step, 0)

    mine = ((z + 1) % nz, (z + nz - 1) % nz)

    def y_copy(d, k):
        return pltpu.make_async_remote_copy(
            src_ref=o_ref.at[d, mine[d], k],
            dst_ref=ybuf.at[d, k],
            send_sem=y_send.at[d, k],
            recv_sem=y_recv.at[d, k],
            device_id=(row, partner),
            device_id_type=MESH,
        )

    for k in range(m):
        for d in range(2):
            y_copy(d, k).start()
    for k in range(m):
        for d in range(2):
            c = y_copy(d, k)
            c.wait_recv()
            c.wait_send()
            o_ref[d, mine[d], k] = o_ref[d, mine[d], k] + ybuf[d, k]

    def rs_drain(s, carry):
        for k in range(m):
            for d in range(2):
                rs_copy(d, s, k).wait_send()
        return carry

    lax.fori_loop(0, nz - 1, rs_drain, 0)
    for nb in (left, right):
        pl.semaphore_signal(ready, inc=1, device_id=(row, nb), device_id_type=MESH)
    pl.semaphore_wait(ready, 2)

    def ag_copy(d, t, k):
        chunk = (z + 1 + nz - t) % nz if d == 0 else (z + nz - 1 + t) % nz
        return pltpu.make_async_remote_copy(
            src_ref=o_ref.at[d, chunk, k],
            dst_ref=o_ref.at[d, chunk, k],
            send_sem=ag_send.at[d, t, k],
            recv_sem=ag_recv.at[d, t, k],
            device_id=(row, peers[d]),
            device_id_type=MESH,
        )

    for k in range(m):
        for d in range(2):
            ag_copy(d, 0, k).start()

    def ag_step(t, carry):
        for k in range(m):
            for d in range(2):
                ag_copy(d, t, k).wait_recv()

                @pl.when(t < nz - 2)
                def _():
                    ag_copy(d, t + 1, k).start()

        return carry

    lax.fori_loop(0, nz - 1, ag_step, 0)

    def drain(s, carry):
        for k in range(m):
            for d in range(2):
                ag_copy(d, s, k).wait_send()
        return carry

    lax.fori_loop(0, nz - 1, drain, 0)


def grid_allreduce(x, cid):
    _, nz, m, rows, cols = x.shape
    return pl.pallas_call(
        functools.partial(grid_kernel, nz, m),
        out_shape=jax.ShapeDtypeStruct(x.shape, x.dtype),
        in_specs=[pl.BlockSpec(memory_space=pltpu.VMEM)],
        out_specs=pl.BlockSpec(memory_space=pltpu.VMEM),
        scratch_shapes=[
            pltpu.VMEM((2, nz - 1, m, rows, cols), x.dtype),
            pltpu.VMEM((2, m, rows, cols), x.dtype),
            pltpu.SemaphoreType.DMA((2, nz - 1, m)),
            pltpu.SemaphoreType.DMA((2, nz - 1, m)),
            pltpu.SemaphoreType.DMA((2, m)),
            pltpu.SemaphoreType.DMA((2, m)),
            pltpu.SemaphoreType.DMA((2, nz - 1, m)),
            pltpu.SemaphoreType.DMA((2, nz - 1, m)),
            pltpu.SemaphoreType.REGULAR,
        ],
        compiler_params=pltpu.CompilerParams(collective_id=cid, has_side_effects=True),
    )(x)


def slot_allreduce(slots, n, cid):
    steps, rows, cols = slots.shape
    total = steps * rows
    sub = 16 if slots.dtype == jnp.bfloat16 else 8
    nz = n // 2
    m = total // (2 * nz * sub)
    out = grid_allreduce(slots.reshape(2, nz, m, sub, cols), cid)
    return out.reshape(steps, rows, cols)


def pair_kernel(scale, group, slabs, flag_ref, q_ref, do_ref, k_ref, v_ref, lse_ref, dot_ref,
                dq_ref, dk_ref, dv_ref, dq_acc):
    h = pl.program_id(0)
    qh = q_ref[...]
    doh = do_ref[...]
    lse = lse_ref[pl.ds(h, 1), :]
    dots = dot_ref[pl.ds(h, 1), :]
    nt = (((1,), (1,)), ((), ()))
    tn = (((0,), (0,)), ((), ()))
    cols = BLK
    dq_acc[...] = jnp.zeros_like(dq_acc)
    for j in range(slabs):
        active = flag_ref[j] > 0

        @pl.when(active)
        def _():
            kj = k_ref[j * cols:(j + 1) * cols, :]
            vj = v_ref[j * cols:(j + 1) * cols, :]
            scores = lax.dot_general(kj, qh, nt, preferred_element_type=jnp.float32) * scale
            probs = jnp.exp(scores - lse)
            if j == 0:
                key_pos = lax.broadcasted_iota(jnp.int32, probs.shape, 0)
                query_pos = lax.broadcasted_iota(jnp.int32, probs.shape, 1)
                probs = jnp.where(key_pos <= query_pos, probs, jnp.float32(0.0))
            grad_probs = lax.dot_general(vj, doh, nt, preferred_element_type=jnp.float32)
            grad_scores = (probs * (grad_probs - dots)).astype(jnp.bfloat16)
            probs_low = probs.astype(jnp.bfloat16)
            dq_acc[...] += lax.dot_general(grad_scores, kj, tn, preferred_element_type=jnp.float32)
            dk = jnp.dot(grad_scores, qh, preferred_element_type=jnp.float32) * scale
            dv = jnp.dot(probs_low, doh, preferred_element_type=jnp.float32)

            @pl.when(h % group == 0)
            def _():
                dk_ref[j] = dk
                dv_ref[j] = dv

            @pl.when(h % group != 0)
            def _():
                dk_ref[j] += dk
                dv_ref[j] += dv

        @pl.when(jnp.logical_not(active) & (h % group == 0))
        def _():
            dk_ref[j] = jnp.zeros(dk_ref.shape[1:], dk_ref.dtype)
            dv_ref[j] = jnp.zeros(dv_ref.shape[1:], dv_ref.dtype)

    dq_ref[...] = (dq_acc[...] * scale).astype(dq_ref.dtype)


def pair_terms(flags, query_rows, grad_rows, norm_rows, dot_rows, key_rows, value_rows):
    rows = query_rows.shape[0]
    cols = key_rows.shape[0]
    slabs = cols // BLK
    group = HQ // HK
    scale = 1.0 / math.sqrt(DH)
    return pl.pallas_call(
        functools.partial(pair_kernel, scale, group, slabs),
        out_shape=(
            jax.ShapeDtypeStruct((rows, HQ * DH), jnp.bfloat16),
            jax.ShapeDtypeStruct((slabs, BLK, HK * DH), jnp.float32),
            jax.ShapeDtypeStruct((slabs, BLK, HK * DH), jnp.float32),
        ),
        grid=(HQ,),
        in_specs=[
            pl.BlockSpec(memory_space=pltpu.SMEM),
            pl.BlockSpec((rows, DH), lambda h: (0, h)),
            pl.BlockSpec((rows, DH), lambda h: (0, h)),
            pl.BlockSpec((cols, DH), lambda h: (0, h // group)),
            pl.BlockSpec((cols, DH), lambda h: (0, h // group)),
            pl.BlockSpec((HQ, rows), lambda h: (0, 0)),
            pl.BlockSpec((HQ, rows), lambda h: (0, 0)),
        ],
        out_specs=[
            pl.BlockSpec((rows, DH), lambda h: (0, h)),
            pl.BlockSpec((slabs, BLK, DH), lambda h: (0, 0, h // group)),
            pl.BlockSpec((slabs, BLK, DH), lambda h: (0, 0, h // group)),
        ],
        scratch_shapes=[pltpu.VMEM((rows, DH), jnp.float32)],
        compiler_params=pltpu.CompilerParams(dimension_semantics=("arbitrary",)),
    )(flags, query_rows, grad_rows, key_rows, value_rows, norm_rows, dot_rows)


def allowed_rows(local_routes, query_start, key_start, tokens, widen, active):
    per_dev = local_routes.shape[0]
    query_blocks = query_start // BLK + jnp.arange(per_dev, dtype=jnp.int32)
    key_blocks = key_start // BLK + jnp.arange(per_dev, dtype=jnp.int32)
    listed = jnp.any(local_routes[:, :, None] == key_blocks[None, None, :], axis=1)
    same = query_blocks[:, None] == key_blocks[None, :]
    chosen = listed & (same | widen) & active
    token_level = jnp.broadcast_to(chosen[:, None, :, None], (per_dev, BLK, per_dev, BLK)).reshape(
        tokens, tokens
    )
    positions = jnp.arange(tokens, dtype=jnp.int32)
    causal = key_start + positions[None, :] <= query_start + positions[:, None]
    return token_level & causal


def make_on_device(n):
    def on_device(
        queries, key_states, value_states, grad_output, log_norms, grad_dots, block_routes, owner_steps
    ):
        tokens = queries.shape[0]
        features = key_states.shape[1]
        device = lax.axis_index("ctx")
        start = device * tokens
        steps = owner_steps.shape[0]
        is_mine = owner_steps == device
        covered = jnp.any(is_mine)
        kv = jnp.concatenate([key_states, value_states], axis=1)
        kv_slots = jnp.where(is_mine[:, None, None], kv[None], jnp.zeros((), kv.dtype))
        kv_all = slot_allreduce(kv_slots, n, 0)
        listed = jnp.any(block_routes[0][None, :] == owner_steps[:, None], axis=1)
        remote = listed & (owner_steps != device) & (owner_steps < device)
        flags = jnp.concatenate([jnp.ones((1,), jnp.int32), remote.astype(jnp.int32)])
        key_cols = jnp.concatenate(
            [key_states, kv_all[:, :, :features].reshape(steps * tokens, features)], axis=0
        )
        value_cols = jnp.concatenate(
            [value_states, kv_all[:, :, features:].reshape(steps * tokens, features)], axis=0
        )
        grad_q, dk_slabs, dv_slabs = pair_terms(
            flags, queries, grad_output, log_norms, grad_dots, key_cols, value_cols
        )
        terms = jnp.concatenate([dk_slabs[1:], dv_slabs[1:]], axis=2)
        summed = slot_allreduce(terms, n, 1)
        held = lax.dynamic_index_in_dim(summed, jnp.argmax(is_mine), keepdims=False)
        held = jnp.where(covered, held, jnp.float32(0.0))
        grad_k = dk_slabs[0] + held[:, :features]
        grad_v = dv_slabs[0] + held[:, features:]
        return (grad_q, grad_k.astype(jnp.bfloat16), grad_v.astype(jnp.bfloat16))

    return on_device


def solution(mesh):
    n = mesh.shape["ctx"]
    return jax.shard_map(
        make_on_device(n),
        mesh=mesh,
        in_specs=(
            P(("dp", "ctx"), None),
            P(("dp", "ctx"), None),
            P(("dp", "ctx"), None),
            P(("dp", "ctx"), None),
            P(None, ("dp", "ctx")),
            P(None, ("dp", "ctx")),
            P(("dp", "ctx"), None),
            P("dp"),
        ),
        out_specs=(P(("dp", "ctx"), None), P(("dp", "ctx"), None), P(("dp", "ctx"), None)),
        check_vma=False,
    )
```

```python
import functools
import math

import jax
import jax.numpy as jnp
from jax import lax
from jax.experimental import pallas as pl
from jax.experimental.pallas import tpu as pltpu
from jax.sharding import PartitionSpec as P

HQ = 16
HK = 4
DH = 128
BLK = 256
MESH = pl.DeviceIdType.MESH


def grid_kernel(nz, m, x_ref, o_ref, rbuf, ybuf, rs_send, rs_recv, y_send, y_recv, ag_send,
                ag_recv, ready):
    me = lax.axis_index("ctx")
    row = lax.axis_index("dp")
    z = me // 2
    y = me % 2
    right = ((z + 1) % nz) * 2 + y
    left = ((z + nz - 1) % nz) * 2 + y
    partner = z * 2 + (1 - y)
    peers = (right, left)

    barrier = pltpu.get_barrier_semaphore()
    for nb in (left, right, partner):
        pl.semaphore_signal(barrier, inc=1, device_id=(row, nb), device_id_type=MESH)
    pl.semaphore_wait(barrier, 3)

    o_ref[...] = x_ref[...]

    def rs_copy(d, s, k):
        send = (z + nz - s) % nz if d == 0 else (z + s) % nz
        return pltpu.make_async_remote_copy(
            src_ref=o_ref.at[d, send, k],
            dst_ref=rbuf.at[d, s, k],
            send_sem=rs_send.at[d, s, k],
            recv_sem=rs_recv.at[d, s, k],
            device_id=(row, peers[d]),
            device_id_type=MESH,
        )

    for k in range(m):
        for d in range(2):
            rs_copy(d, 0, k).start()

    def rs_step(s, carry):
        for k in range(m):
            for d in range(2):
                rs_copy(d, s, k).wait_recv()
                got = (z + 2 * nz - s - 1) % nz if d == 0 else (z + s + 1) % nz
                o_ref[d, got, k] = o_ref[d, got, k] + rbuf[d, s, k]

                @pl.when(s < nz - 2)
                def _():
                    rs_copy(d, s + 1, k).start()

        return carry

    lax.fori_loop(0, nz - 1, rs_step, 0)

    mine = ((z + 1) % nz, (z + nz - 1) % nz)

    def y_copy(d, k):
        return pltpu.make_async_remote_copy(
            src_ref=o_ref.at[d, mine[d], k],
            dst_ref=ybuf.at[d, k],
            send_sem=y_send.at[d, k],
            recv_sem=y_recv.at[d, k],
            device_id=(row, partner),
            device_id_type=MESH,
        )

    for k in range(m):
        for d in range(2):
            y_copy(d, k).start()
    for k in range(m):
        for d in range(2):
            c = y_copy(d, k)
            c.wait_recv()
            c.wait_send()
            o_ref[d, mine[d], k] = o_ref[d, mine[d], k] + ybuf[d, k]

    def rs_drain(s, carry):
        for k in range(m):
            for d in range(2):
                rs_copy(d, s, k).wait_send()
        return carry

    lax.fori_loop(0, nz - 1, rs_drain, 0)
    for nb in (left, right):
        pl.semaphore_signal(ready, inc=1, device_id=(row, nb), device_id_type=MESH)
    pl.semaphore_wait(ready, 2)

    def ag_copy(d, t, k):
        chunk = (z + 1 + nz - t) % nz if d == 0 else (z + nz - 1 + t) % nz
        return pltpu.make_async_remote_copy(
            src_ref=o_ref.at[d, chunk, k],
            dst_ref=o_ref.at[d, chunk, k],
            send_sem=ag_send.at[d, t, k],
            recv_sem=ag_recv.at[d, t, k],
            device_id=(row, peers[d]),
            device_id_type=MESH,
        )

    for k in range(m):
        for d in range(2):
            ag_copy(d, 0, k).start()

    def ag_step(t, carry):
        for k in range(m):
            for d in range(2):
                ag_copy(d, t, k).wait_recv()

                @pl.when(t < nz - 2)
                def _():
                    ag_copy(d, t + 1, k).start()

        return carry

    lax.fori_loop(0, nz - 1, ag_step, 0)

    def drain(s, carry):
        for k in range(m):
            for d in range(2):
                ag_copy(d, s, k).wait_send()
        return carry

    lax.fori_loop(0, nz - 1, drain, 0)


def grid_allreduce(x, cid):
    _, nz, m, rows, cols = x.shape
    return pl.pallas_call(
        functools.partial(grid_kernel, nz, m),
        out_shape=jax.ShapeDtypeStruct(x.shape, x.dtype),
        in_specs=[pl.BlockSpec(memory_space=pltpu.VMEM)],
        out_specs=pl.BlockSpec(memory_space=pltpu.VMEM),
        scratch_shapes=[
            pltpu.VMEM((2, nz - 1, m, rows, cols), x.dtype),
            pltpu.VMEM((2, m, rows, cols), x.dtype),
            pltpu.SemaphoreType.DMA((2, nz - 1, m)),
            pltpu.SemaphoreType.DMA((2, nz - 1, m)),
            pltpu.SemaphoreType.DMA((2, m)),
            pltpu.SemaphoreType.DMA((2, m)),
            pltpu.SemaphoreType.DMA((2, nz - 1, m)),
            pltpu.SemaphoreType.DMA((2, nz - 1, m)),
            pltpu.SemaphoreType.REGULAR,
        ],
        compiler_params=pltpu.CompilerParams(collective_id=cid, has_side_effects=True),
    )(x)


def slot_allreduce(slots, n, cid):
    steps, rows, cols = slots.shape
    total = steps * rows
    sub = 16 if slots.dtype == jnp.bfloat16 else 8
    nz = n // 2
    m = total // (2 * nz * sub)
    out = grid_allreduce(slots.reshape(2, nz, m, sub, cols), cid)
    return out.reshape(steps, rows, cols)


def pair_kernel(scale, group, flag_ref, q_ref, do_ref, k_ref, v_ref, lse_ref, dot_ref, dq_ref,
                dk_ref, dv_ref, mask_ref):
    h = pl.program_id(0)

    @pl.when(h == 0)
    def _():
        key_pos = lax.broadcasted_iota(jnp.int32, (BLK, BLK), 0)
        query_pos = lax.broadcasted_iota(jnp.int32, (BLK, BLK), 1)
        mask_ref[0:BLK, :] = jnp.where(key_pos <= query_pos, jnp.float32(1.0), jnp.float32(0.0))
        for j in range(1, mask_ref.shape[0] // BLK):
            mask_ref[j * BLK:(j + 1) * BLK, :] = jnp.full(
                (BLK, mask_ref.shape[1]), flag_ref[j].astype(jnp.float32), jnp.float32
            )

    qh = q_ref[...]
    doh = do_ref[...]
    kg = k_ref[...]
    vg = v_ref[...]
    nt = (((1,), (1,)), ((), ()))
    scores = lax.dot_general(kg, qh, nt, preferred_element_type=jnp.float32) * scale
    lse = lse_ref[pl.ds(h, 1), :]
    dots = dot_ref[pl.ds(h, 1), :]
    probs = jnp.where(mask_ref[...] > 0, jnp.exp(scores - lse), jnp.float32(0.0))
    grad_probs = lax.dot_general(vg, doh, nt, preferred_element_type=jnp.float32)
    grad_scores = (probs * (grad_probs - dots)).astype(jnp.bfloat16)
    probs_low = probs.astype(jnp.bfloat16)
    tn = (((0,), (0,)), ((), ()))
    dq = lax.dot_general(grad_scores, kg, tn, preferred_element_type=jnp.float32) * scale
    dq_ref[...] = dq.astype(dq_ref.dtype)
    dk = jnp.dot(grad_scores, qh, preferred_element_type=jnp.float32) * scale
    dv = jnp.dot(probs_low, doh, preferred_element_type=jnp.float32)

    @pl.when(h % group == 0)
    def _():
        dk_ref[...] = dk
        dv_ref[...] = dv

    @pl.when(h % group != 0)
    def _():
        dk_ref[...] += dk
        dv_ref[...] += dv


def pair_terms(flags, query_rows, grad_rows, norm_rows, dot_rows, key_rows, value_rows):
    rows = query_rows.shape[0]
    cols = key_rows.shape[0]
    group = HQ // HK
    scale = 1.0 / math.sqrt(DH)
    return pl.pallas_call(
        functools.partial(pair_kernel, scale, group),
        out_shape=(
            jax.ShapeDtypeStruct((rows, HQ * DH), jnp.bfloat16),
            jax.ShapeDtypeStruct((cols, HK * DH), jnp.float32),
            jax.ShapeDtypeStruct((cols, HK * DH), jnp.float32),
        ),
        grid=(HQ,),
        in_specs=[
            pl.BlockSpec(memory_space=pltpu.SMEM),
            pl.BlockSpec((rows, DH), lambda h: (0, h)),
            pl.BlockSpec((rows, DH), lambda h: (0, h)),
            pl.BlockSpec((cols, DH), lambda h: (0, h // group)),
            pl.BlockSpec((cols, DH), lambda h: (0, h // group)),
            pl.BlockSpec((HQ, rows), lambda h: (0, 0)),
            pl.BlockSpec((HQ, rows), lambda h: (0, 0)),
        ],
        out_specs=[
            pl.BlockSpec((rows, DH), lambda h: (0, h)),
            pl.BlockSpec((cols, DH), lambda h: (0, h // group)),
            pl.BlockSpec((cols, DH), lambda h: (0, h // group)),
        ],
        scratch_shapes=[pltpu.VMEM((cols, rows), jnp.float32)],
        compiler_params=pltpu.CompilerParams(dimension_semantics=("arbitrary",)),
    )(flags, query_rows, grad_rows, key_rows, value_rows, norm_rows, dot_rows)


def allowed_rows(local_routes, query_start, key_start, tokens, widen, active):
    per_dev = local_routes.shape[0]
    query_blocks = query_start // BLK + jnp.arange(per_dev, dtype=jnp.int32)
    key_blocks = key_start // BLK + jnp.arange(per_dev, dtype=jnp.int32)
    listed = jnp.any(local_routes[:, :, None] == key_blocks[None, None, :], axis=1)
    same = query_blocks[:, None] == key_blocks[None, :]
    chosen = listed & (same | widen) & active
    token_level = jnp.broadcast_to(chosen[:, None, :, None], (per_dev, BLK, per_dev, BLK)).reshape(
        tokens, tokens
    )
    positions = jnp.arange(tokens, dtype=jnp.int32)
    causal = key_start + positions[None, :] <= query_start + positions[:, None]
    return token_level & causal


def make_on_device(n):
    def on_device(
        queries, key_states, value_states, grad_output, log_norms, grad_dots, block_routes, owner_steps
    ):
        tokens = queries.shape[0]
        features = key_states.shape[1]
        device = lax.axis_index("ctx")
        start = device * tokens
        steps = owner_steps.shape[0]
        is_mine = owner_steps == device
        covered = jnp.any(is_mine)
        kv = jnp.concatenate([key_states, value_states], axis=1)
        kv_slots = jnp.where(is_mine[:, None, None], kv[None], jnp.zeros((), kv.dtype))
        kv_all = slot_allreduce(kv_slots, n, 0)
        listed = jnp.any(block_routes[0][None, :] == owner_steps[:, None], axis=1)
        remote = listed & (owner_steps != device) & (owner_steps < device)
        flags = jnp.concatenate([jnp.ones((1,), jnp.int32), remote.astype(jnp.int32)])
        key_cols = jnp.concatenate(
            [key_states, kv_all[:, :, :features].reshape(steps * tokens, features)], axis=0
        )
        value_cols = jnp.concatenate(
            [value_states, kv_all[:, :, features:].reshape(steps * tokens, features)], axis=0
        )
        grad_q, grad_k_all, grad_v_all = pair_terms(
            flags, queries, grad_output, log_norms, grad_dots, key_cols, value_cols
        )
        terms = jnp.concatenate(
            [
                grad_k_all[tokens:].reshape(steps, tokens, features),
                grad_v_all[tokens:].reshape(steps, tokens, features),
            ],
            axis=2,
        )
        summed = slot_allreduce(terms, n, 1)
        held = lax.dynamic_index_in_dim(summed, jnp.argmax(is_mine), keepdims=False)
        held = jnp.where(covered, held, jnp.float32(0.0))
        grad_k = grad_k_all[:tokens] + held[:, :features]
        grad_v = grad_v_all[:tokens] + held[:, features:]
        return (grad_q, grad_k.astype(jnp.bfloat16), grad_v.astype(jnp.bfloat16))

    return on_device


def solution(mesh):
    n = mesh.shape["ctx"]
    return jax.shard_map(
        make_on_device(n),
        mesh=mesh,
        in_specs=(
            P(("dp", "ctx"), None),
            P(("dp", "ctx"), None),
            P(("dp", "ctx"), None),
            P(("dp", "ctx"), None),
            P(None, ("dp", "ctx")),
            P(None, ("dp", "ctx")),
            P(("dp", "ctx"), None),
            P("dp"),
        ),
        out_specs=(P(("dp", "ctx"), None), P(("dp", "ctx"), None), P(("dp", "ctx"), None)),
        check_vma=False,
    )
```

```python
import functools
import math

import jax
import jax.numpy as jnp
from jax import lax
from jax.experimental import pallas as pl
from jax.experimental.pallas import tpu as pltpu
from jax.sharding import PartitionSpec as P

HQ = 16
HK = 4
DH = 128
BLK = 256
MESH = pl.DeviceIdType.MESH


def grid_kernel(nz, m, x_ref, o_ref, rbuf, ybuf, rs_send, rs_recv, y_send, y_recv, ag_send,
                ag_recv, ready):
    me = lax.axis_index("ctx")
    row = lax.axis_index("dp")
    z = me // 2
    y = me % 2
    right = ((z + 1) % nz) * 2 + y
    left = ((z + nz - 1) % nz) * 2 + y
    partner = z * 2 + (1 - y)
    peers = (right, left)

    barrier = pltpu.get_barrier_semaphore()
    for nb in (left, right, partner):
        pl.semaphore_signal(barrier, inc=1, device_id=(row, nb), device_id_type=MESH)
    pl.semaphore_wait(barrier, 3)

    o_ref[...] = x_ref[...]

    def rs_copy(d, s, k):
        send = (z + nz - s) % nz if d == 0 else (z + s) % nz
        return pltpu.make_async_remote_copy(
            src_ref=o_ref.at[d, send, k],
            dst_ref=rbuf.at[d, s, k],
            send_sem=rs_send.at[d, s, k],
            recv_sem=rs_recv.at[d, s, k],
            device_id=(row, peers[d]),
            device_id_type=MESH,
        )

    for k in range(m):
        for d in range(2):
            rs_copy(d, 0, k).start()

    def rs_step(s, carry):
        for k in range(m):
            for d in range(2):
                rs_copy(d, s, k).wait_recv()
                got = (z + 2 * nz - s - 1) % nz if d == 0 else (z + s + 1) % nz
                o_ref[d, got, k] = o_ref[d, got, k] + rbuf[d, s, k]

                @pl.when(s < nz - 2)
                def _():
                    rs_copy(d, s + 1, k).start()

        return carry

    lax.fori_loop(0, nz - 1, rs_step, 0)

    mine = ((z + 1) % nz, (z + nz - 1) % nz)

    def y_copy(d, k):
        return pltpu.make_async_remote_copy(
            src_ref=o_ref.at[d, mine[d], k],
            dst_ref=ybuf.at[d, k],
            send_sem=y_send.at[d, k],
            recv_sem=y_recv.at[d, k],
            device_id=(row, partner),
            device_id_type=MESH,
        )

    for k in range(m):
        for d in range(2):
            y_copy(d, k).start()
    for k in range(m):
        for d in range(2):
            c = y_copy(d, k)
            c.wait_recv()
            c.wait_send()
            o_ref[d, mine[d], k] = o_ref[d, mine[d], k] + ybuf[d, k]

    def rs_drain(s, carry):
        for k in range(m):
            for d in range(2):
                rs_copy(d, s, k).wait_send()
        return carry

    lax.fori_loop(0, nz - 1, rs_drain, 0)
    for nb in (left, right):
        pl.semaphore_signal(ready, inc=1, device_id=(row, nb), device_id_type=MESH)
    pl.semaphore_wait(ready, 2)

    def ag_copy(d, t, k):
        chunk = (z + 1 + nz - t) % nz if d == 0 else (z + nz - 1 + t) % nz
        return pltpu.make_async_remote_copy(
            src_ref=o_ref.at[d, chunk, k],
            dst_ref=o_ref.at[d, chunk, k],
            send_sem=ag_send.at[d, t, k],
            recv_sem=ag_recv.at[d, t, k],
            device_id=(row, peers[d]),
            device_id_type=MESH,
        )

    for k in range(m):
        for d in range(2):
            ag_copy(d, 0, k).start()

    def ag_step(t, carry):
        for k in range(m):
            for d in range(2):
                ag_copy(d, t, k).wait_recv()

                @pl.when(t < nz - 2)
                def _():
                    ag_copy(d, t + 1, k).start()

        return carry

    lax.fori_loop(0, nz - 1, ag_step, 0)

    def drain(s, carry):
        for k in range(m):
            for d in range(2):
                ag_copy(d, s, k).wait_send()
        return carry

    lax.fori_loop(0, nz - 1, drain, 0)


def grid_allreduce(x, cid):
    _, nz, m, rows, cols = x.shape
    return pl.pallas_call(
        functools.partial(grid_kernel, nz, m),
        out_shape=jax.ShapeDtypeStruct(x.shape, x.dtype),
        in_specs=[pl.BlockSpec(memory_space=pltpu.VMEM)],
        out_specs=pl.BlockSpec(memory_space=pltpu.VMEM),
        scratch_shapes=[
            pltpu.VMEM((2, nz - 1, m, rows, cols), x.dtype),
            pltpu.VMEM((2, m, rows, cols), x.dtype),
            pltpu.SemaphoreType.DMA((2, nz - 1, m)),
            pltpu.SemaphoreType.DMA((2, nz - 1, m)),
            pltpu.SemaphoreType.DMA((2, m)),
            pltpu.SemaphoreType.DMA((2, m)),
            pltpu.SemaphoreType.DMA((2, nz - 1, m)),
            pltpu.SemaphoreType.DMA((2, nz - 1, m)),
            pltpu.SemaphoreType.REGULAR,
        ],
        compiler_params=pltpu.CompilerParams(collective_id=cid, has_side_effects=True),
    )(x)


def slot_allreduce(slots, n, cid):
    steps, rows, cols = slots.shape
    total = steps * rows
    sub = 16 if slots.dtype == jnp.bfloat16 else 8
    nz = n // 2
    m = total // (2 * nz * sub)
    out = grid_allreduce(slots.reshape(2, nz, m, sub, cols), cid)
    return out.reshape(steps, rows, cols)


def pair_kernel(scale, group, flag_ref, q_ref, do_ref, k_ref, v_ref, kv_ref, lse_ref, dot_ref,
                dq_ref, dk_ref, dv_ref, terms_ref, mask_ref):
    h = pl.program_id(0)
    g = h // group
    steps, tokens, width = kv_ref.shape
    features = width // 2

    @pl.when(h == 0)
    def _():
        key_pos = lax.broadcasted_iota(jnp.int32, (BLK, BLK), 0)
        query_pos = lax.broadcasted_iota(jnp.int32, (BLK, BLK), 1)
        mask_ref[0:BLK, :] = jnp.where(key_pos <= query_pos, jnp.float32(1.0), jnp.float32(0.0))
        for j in range(1, mask_ref.shape[0] // BLK):
            mask_ref[j * BLK:(j + 1) * BLK, :] = jnp.full(
                (BLK, mask_ref.shape[1]), flag_ref[j].astype(jnp.float32), jnp.float32
            )

    k_lane = pl.ds(pl.multiple_of(g * DH, DH), DH)
    v_lane = pl.ds(pl.multiple_of(features + g * DH, DH), DH)
    qh = q_ref[...]
    doh = do_ref[...]
    kg = jnp.concatenate([k_ref[...], kv_ref[:, :, k_lane].reshape(steps * tokens, DH)], axis=0)
    vg = jnp.concatenate([v_ref[...], kv_ref[:, :, v_lane].reshape(steps * tokens, DH)], axis=0)
    nt = (((1,), (1,)), ((), ()))
    scores = lax.dot_general(kg, qh, nt, preferred_element_type=jnp.float32) * scale
    lse = lse_ref[pl.ds(h, 1), :]
    dots = dot_ref[pl.ds(h, 1), :]
    probs = jnp.where(mask_ref[...] > 0, jnp.exp(scores - lse), jnp.float32(0.0))
    grad_probs = lax.dot_general(vg, doh, nt, preferred_element_type=jnp.float32)
    grad_scores = (probs * (grad_probs - dots)).astype(jnp.bfloat16)
    probs_low = probs.astype(jnp.bfloat16)
    tn = (((0,), (0,)), ((), ()))
    dq = lax.dot_general(grad_scores, kg, tn, preferred_element_type=jnp.float32) * scale
    dq_ref[...] = dq.astype(dq_ref.dtype)
    dk = jnp.dot(grad_scores, qh, preferred_element_type=jnp.float32) * scale
    dv = jnp.dot(probs_low, doh, preferred_element_type=jnp.float32)
    dk_far = dk[tokens:].reshape(steps, tokens, DH)
    dv_far = dv[tokens:].reshape(steps, tokens, DH)

    @pl.when(h % group == 0)
    def _():
        dk_ref[...] = dk[:tokens]
        dv_ref[...] = dv[:tokens]
        terms_ref[:, :, k_lane] = dk_far
        terms_ref[:, :, v_lane] = dv_far

    @pl.when(h % group != 0)
    def _():
        dk_ref[...] += dk[:tokens]
        dv_ref[...] += dv[:tokens]
        terms_ref[:, :, k_lane] += dk_far
        terms_ref[:, :, v_lane] += dv_far


def pair_terms(flags, query_rows, grad_rows, norm_rows, dot_rows, key_rows, value_rows, kv_all):
    rows = query_rows.shape[0]
    tokens = key_rows.shape[0]
    steps, _, width = kv_all.shape
    cols = tokens * (1 + steps)
    group = HQ // HK
    scale = 1.0 / math.sqrt(DH)
    return pl.pallas_call(
        functools.partial(pair_kernel, scale, group),
        out_shape=(
            jax.ShapeDtypeStruct((rows, HQ * DH), jnp.bfloat16),
            jax.ShapeDtypeStruct((tokens, HK * DH), jnp.float32),
            jax.ShapeDtypeStruct((tokens, HK * DH), jnp.float32),
            jax.ShapeDtypeStruct((steps, tokens, width), jnp.float32),
        ),
        grid=(HQ,),
        in_specs=[
            pl.BlockSpec(memory_space=pltpu.SMEM),
            pl.BlockSpec((rows, DH), lambda h: (0, h)),
            pl.BlockSpec((rows, DH), lambda h: (0, h)),
            pl.BlockSpec((tokens, DH), lambda h: (0, h // group)),
            pl.BlockSpec((tokens, DH), lambda h: (0, h // group)),
            pl.BlockSpec((steps, tokens, width), lambda h: (0, 0, 0)),
            pl.BlockSpec((HQ, rows), lambda h: (0, 0)),
            pl.BlockSpec((HQ, rows), lambda h: (0, 0)),
        ],
        out_specs=[
            pl.BlockSpec((rows, DH), lambda h: (0, h)),
            pl.BlockSpec((tokens, DH), lambda h: (0, h // group)),
            pl.BlockSpec((tokens, DH), lambda h: (0, h // group)),
            pl.BlockSpec((steps, tokens, width), lambda h: (0, 0, 0)),
        ],
        scratch_shapes=[pltpu.VMEM((cols, rows), jnp.float32)],
        compiler_params=pltpu.CompilerParams(dimension_semantics=("arbitrary",)),
    )(flags, query_rows, grad_rows, key_rows, value_rows, kv_all, norm_rows, dot_rows)


def allowed_rows(local_routes, query_start, key_start, tokens, widen, active):
    per_dev = local_routes.shape[0]
    query_blocks = query_start // BLK + jnp.arange(per_dev, dtype=jnp.int32)
    key_blocks = key_start // BLK + jnp.arange(per_dev, dtype=jnp.int32)
    listed = jnp.any(local_routes[:, :, None] == key_blocks[None, None, :], axis=1)
    same = query_blocks[:, None] == key_blocks[None, :]
    chosen = listed & (same | widen) & active
    token_level = jnp.broadcast_to(chosen[:, None, :, None], (per_dev, BLK, per_dev, BLK)).reshape(
        tokens, tokens
    )
    positions = jnp.arange(tokens, dtype=jnp.int32)
    causal = key_start + positions[None, :] <= query_start + positions[:, None]
    return token_level & causal


def make_on_device(n):
    def on_device(
        queries, key_states, value_states, grad_output, log_norms, grad_dots, block_routes, owner_steps
    ):
        tokens = queries.shape[0]
        features = key_states.shape[1]
        device = lax.axis_index("ctx")
        start = device * tokens
        steps = owner_steps.shape[0]
        is_mine = owner_steps == device
        covered = jnp.any(is_mine)
        kv = jnp.concatenate([key_states, value_states], axis=1)
        kv_slots = jnp.where(is_mine[:, None, None], kv[None], jnp.zeros((), kv.dtype))
        kv_all = slot_allreduce(kv_slots, n, 0)
        listed = jnp.any(block_routes[0][None, :] == owner_steps[:, None], axis=1)
        remote = listed & (owner_steps != device) & (owner_steps < device)
        flags = jnp.concatenate([jnp.ones((1,), jnp.int32), remote.astype(jnp.int32)])
        grad_q, grad_k, grad_v, terms = pair_terms(
            flags, queries, grad_output, log_norms, grad_dots, key_states, value_states, kv_all
        )
        summed = slot_allreduce(terms, n, 1)
        held = lax.dynamic_index_in_dim(summed, jnp.argmax(is_mine), keepdims=False)
        held = jnp.where(covered, held, jnp.float32(0.0))
        grad_k = grad_k + held[:, :features]
        grad_v = grad_v + held[:, features:]
        return (grad_q, grad_k.astype(jnp.bfloat16), grad_v.astype(jnp.bfloat16))

    return on_device


def solution(mesh):
    n = mesh.shape["ctx"]
    return jax.shard_map(
        make_on_device(n),
        mesh=mesh,
        in_specs=(
            P(("dp", "ctx"), None),
            P(("dp", "ctx"), None),
            P(("dp", "ctx"), None),
            P(("dp", "ctx"), None),
            P(None, ("dp", "ctx")),
            P(None, ("dp", "ctx")),
            P(("dp", "ctx"), None),
            P("dp"),
        ),
        out_specs=(P(("dp", "ctx"), None), P(("dp", "ctx"), None), P(("dp", "ctx"), None)),
        check_vma=False,
    )
```

```python
import functools
import math

import jax
import jax.numpy as jnp
from jax import lax
from jax.experimental import pallas as pl
from jax.experimental.pallas import tpu as pltpu
from jax.sharding import PartitionSpec as P

HQ = 16
HK = 4
DH = 128
BLK = 256
MESH = pl.DeviceIdType.MESH


def grid_kernel(nz, m, n_in, *refs):
    ins = refs[:n_in]
    o_ref, rbuf, ybuf, rs_send, rs_recv, y_send, y_recv, ag_send, ag_recv, ready = refs[n_in:]
    me = lax.axis_index("ctx")
    row = lax.axis_index("dp")
    z = me // 2
    y = me % 2
    right = ((z + 1) % nz) * 2 + y
    left = ((z + nz - 1) % nz) * 2 + y
    partner = z * 2 + (1 - y)
    peers = (right, left)

    barrier = pltpu.get_barrier_semaphore()
    for nb in (left, right, partner):
        pl.semaphore_signal(barrier, inc=1, device_id=(row, nb), device_id_type=MESH)
    pl.semaphore_wait(barrier, 3)

    if n_in == 1:
        o_ref[...] = ins[0][...]
    else:
        flag_ref, kv_ref = ins
        per = kv_ref.shape[0]
        for i in range(flag_ref.shape[0]):
            d, c = divmod(i * per, nz)
            o_ref[d, c:c + per] = jnp.where(flag_ref[i] > 0, kv_ref[...], jnp.zeros((), kv_ref.dtype))

    def rs_copy(d, s, k):
        send = (z + nz - s) % nz if d == 0 else (z + s) % nz
        return pltpu.make_async_remote_copy(
            src_ref=o_ref.at[d, send, k],
            dst_ref=rbuf.at[d, s, k],
            send_sem=rs_send.at[d, s, k],
            recv_sem=rs_recv.at[d, s, k],
            device_id=(row, peers[d]),
            device_id_type=MESH,
        )

    for k in range(m):
        for d in range(2):
            rs_copy(d, 0, k).start()

    def rs_step(s, carry):
        for k in range(m):
            for d in range(2):
                rs_copy(d, s, k).wait_recv()
                got = (z + 2 * nz - s - 1) % nz if d == 0 else (z + s + 1) % nz
                o_ref[d, got, k] = o_ref[d, got, k] + rbuf[d, s, k]

                @pl.when(s < nz - 2)
                def _():
                    rs_copy(d, s + 1, k).start()

        return carry

    lax.fori_loop(0, nz - 1, rs_step, 0)

    mine = ((z + 1) % nz, (z + nz - 1) % nz)

    def y_copy(d, k):
        return pltpu.make_async_remote_copy(
            src_ref=o_ref.at[d, mine[d], k],
            dst_ref=ybuf.at[d, k],
            send_sem=y_send.at[d, k],
            recv_sem=y_recv.at[d, k],
            device_id=(row, partner),
            device_id_type=MESH,
        )

    for k in range(m):
        for d in range(2):
            y_copy(d, k).start()
    for k in range(m):
        for d in range(2):
            c = y_copy(d, k)
            c.wait_recv()
            c.wait_send()
            o_ref[d, mine[d], k] = o_ref[d, mine[d], k] + ybuf[d, k]

    def rs_drain(s, carry):
        for k in range(m):
            for d in range(2):
                rs_copy(d, s, k).wait_send()
        return carry

    lax.fori_loop(0, nz - 1, rs_drain, 0)
    for nb in (left, right):
        pl.semaphore_signal(ready, inc=1, device_id=(row, nb), device_id_type=MESH)
    pl.semaphore_wait(ready, 2)

    def ag_copy(d, t, k):
        chunk = (z + 1 + nz - t) % nz if d == 0 else (z + nz - 1 + t) % nz
        return pltpu.make_async_remote_copy(
            src_ref=o_ref.at[d, chunk, k],
            dst_ref=o_ref.at[d, chunk, k],
            send_sem=ag_send.at[d, t, k],
            recv_sem=ag_recv.at[d, t, k],
            device_id=(row, peers[d]),
            device_id_type=MESH,
        )

    for k in range(m):
        for d in range(2):
            ag_copy(d, 0, k).start()

    def ag_step(t, carry):
        for k in range(m):
            for d in range(2):
                ag_copy(d, t, k).wait_recv()

                @pl.when(t < nz - 2)
                def _():
                    ag_copy(d, t + 1, k).start()

        return carry

    lax.fori_loop(0, nz - 1, ag_step, 0)

    def drain(s, carry):
        for k in range(m):
            for d in range(2):
                ag_copy(d, s, k).wait_send()
        return carry

    lax.fori_loop(0, nz - 1, drain, 0)


def grid_allreduce(x, cid, shape=None, flags=None):
    shape = x.shape if shape is None else shape
    _, nz, m, rows, cols = shape
    ins = (x,) if flags is None else (flags, x)
    specs = [pl.BlockSpec(memory_space=pltpu.VMEM)]
    if flags is not None:
        specs = [pl.BlockSpec(memory_space=pltpu.SMEM)] + specs
    return pl.pallas_call(
        functools.partial(grid_kernel, nz, m, len(ins)),
        out_shape=jax.ShapeDtypeStruct(shape, x.dtype),
        in_specs=specs,
        out_specs=pl.BlockSpec(memory_space=pltpu.VMEM),
        scratch_shapes=[
            pltpu.VMEM((2, nz - 1, m, rows, cols), x.dtype),
            pltpu.VMEM((2, m, rows, cols), x.dtype),
            pltpu.SemaphoreType.DMA((2, nz - 1, m)),
            pltpu.SemaphoreType.DMA((2, nz - 1, m)),
            pltpu.SemaphoreType.DMA((2, m)),
            pltpu.SemaphoreType.DMA((2, m)),
            pltpu.SemaphoreType.DMA((2, nz - 1, m)),
            pltpu.SemaphoreType.DMA((2, nz - 1, m)),
            pltpu.SemaphoreType.REGULAR,
        ],
        compiler_params=pltpu.CompilerParams(collective_id=cid, has_side_effects=True),
    )(*ins)


def slot_allreduce(slots, n, cid):
    steps, rows, cols = slots.shape
    total = steps * rows
    sub = 16 if slots.dtype == jnp.bfloat16 else 8
    nz = n // 2
    m = total // (2 * nz * sub)
    out = grid_allreduce(slots.reshape(2, nz, m, sub, cols), cid)
    return out.reshape(steps, rows, cols)


def pair_kernel(scale, group, flag_ref, q_ref, do_ref, k_ref, v_ref, kv_ref, lse_ref, dot_ref,
                dq_ref, dk_ref, dv_ref, terms_ref, mask_ref):
    h = pl.program_id(0)
    g = h // group
    steps, tokens, width = kv_ref.shape
    features = width // 2

    @pl.when(h == 0)
    def _():
        key_pos = lax.broadcasted_iota(jnp.int32, (BLK, BLK), 0)
        query_pos = lax.broadcasted_iota(jnp.int32, (BLK, BLK), 1)
        mask_ref[0:BLK, :] = jnp.where(key_pos <= query_pos, jnp.float32(1.0), jnp.float32(0.0))
        for j in range(1, mask_ref.shape[0] // BLK):
            mask_ref[j * BLK:(j + 1) * BLK, :] = jnp.full(
                (BLK, mask_ref.shape[1]), flag_ref[j].astype(jnp.float32), jnp.float32
            )

    k_lane = pl.ds(pl.multiple_of(g * DH, DH), DH)
    v_lane = pl.ds(pl.multiple_of(features + g * DH, DH), DH)
    qh = q_ref[...]
    doh = do_ref[...]
    kg = jnp.concatenate([k_ref[...], kv_ref[:, :, k_lane].reshape(steps * tokens, DH)], axis=0)
    vg = jnp.concatenate([v_ref[...], kv_ref[:, :, v_lane].reshape(steps * tokens, DH)], axis=0)
    nt = (((1,), (1,)), ((), ()))
    scores = lax.dot_general(kg, qh, nt, preferred_element_type=jnp.float32) * scale
    lse = lse_ref[pl.ds(h, 1), :]
    dots = dot_ref[pl.ds(h, 1), :]
    probs = jnp.where(mask_ref[...] > 0, jnp.exp(scores - lse), jnp.float32(0.0))
    grad_probs = lax.dot_general(vg, doh, nt, preferred_element_type=jnp.float32)
    grad_scores = (probs * (grad_probs - dots)).astype(jnp.bfloat16)
    probs_low = probs.astype(jnp.bfloat16)
    tn = (((0,), (0,)), ((), ()))
    dq = lax.dot_general(grad_scores, kg, tn, preferred_element_type=jnp.float32) * scale
    dq_ref[...] = dq.astype(dq_ref.dtype)
    dk = jnp.dot(grad_scores, qh, preferred_element_type=jnp.float32) * scale
    dv = jnp.dot(probs_low, doh, preferred_element_type=jnp.float32)
    dk_far = dk[tokens:].reshape(steps, tokens, DH)
    dv_far = dv[tokens:].reshape(steps, tokens, DH)

    @pl.when(h % group == 0)
    def _():
        dk_ref[...] = dk[:tokens]
        dv_ref[...] = dv[:tokens]
        terms_ref[:, :, k_lane] = dk_far
        terms_ref[:, :, v_lane] = dv_far

    @pl.when(h % group != 0)
    def _():
        dk_ref[...] += dk[:tokens]
        dv_ref[...] += dv[:tokens]
        terms_ref[:, :, k_lane] += dk_far
        terms_ref[:, :, v_lane] += dv_far


def pair_terms(flags, query_rows, grad_rows, norm_rows, dot_rows, key_rows, value_rows, kv_all):
    rows = query_rows.shape[0]
    tokens = key_rows.shape[0]
    steps, _, width = kv_all.shape
    cols = tokens * (1 + steps)
    group = HQ // HK
    scale = 1.0 / math.sqrt(DH)
    return pl.pallas_call(
        functools.partial(pair_kernel, scale, group),
        out_shape=(
            jax.ShapeDtypeStruct((rows, HQ * DH), jnp.bfloat16),
            jax.ShapeDtypeStruct((tokens, HK * DH), jnp.float32),
            jax.ShapeDtypeStruct((tokens, HK * DH), jnp.float32),
            jax.ShapeDtypeStruct((steps, tokens, width), jnp.float32),
        ),
        grid=(HQ,),
        in_specs=[
            pl.BlockSpec(memory_space=pltpu.SMEM),
            pl.BlockSpec((rows, DH), lambda h: (0, h)),
            pl.BlockSpec((rows, DH), lambda h: (0, h)),
            pl.BlockSpec((tokens, DH), lambda h: (0, h // group)),
            pl.BlockSpec((tokens, DH), lambda h: (0, h // group)),
            pl.BlockSpec((steps, tokens, width), lambda h: (0, 0, 0)),
            pl.BlockSpec((HQ, rows), lambda h: (0, 0)),
            pl.BlockSpec((HQ, rows), lambda h: (0, 0)),
        ],
        out_specs=[
            pl.BlockSpec((rows, DH), lambda h: (0, h)),
            pl.BlockSpec((tokens, DH), lambda h: (0, h // group)),
            pl.BlockSpec((tokens, DH), lambda h: (0, h // group)),
            pl.BlockSpec((steps, tokens, width), lambda h: (0, 0, 0)),
        ],
        scratch_shapes=[pltpu.VMEM((cols, rows), jnp.float32)],
        compiler_params=pltpu.CompilerParams(dimension_semantics=("arbitrary",)),
    )(flags, query_rows, grad_rows, key_rows, value_rows, kv_all, norm_rows, dot_rows)


def allowed_rows(local_routes, query_start, key_start, tokens, widen, active):
    per_dev = local_routes.shape[0]
    query_blocks = query_start // BLK + jnp.arange(per_dev, dtype=jnp.int32)
    key_blocks = key_start // BLK + jnp.arange(per_dev, dtype=jnp.int32)
    listed = jnp.any(local_routes[:, :, None] == key_blocks[None, None, :], axis=1)
    same = query_blocks[:, None] == key_blocks[None, :]
    chosen = listed & (same | widen) & active
    token_level = jnp.broadcast_to(chosen[:, None, :, None], (per_dev, BLK, per_dev, BLK)).reshape(
        tokens, tokens
    )
    positions = jnp.arange(tokens, dtype=jnp.int32)
    causal = key_start + positions[None, :] <= query_start + positions[:, None]
    return token_level & causal


def make_on_device(n):
    def on_device(
        queries, key_states, value_states, grad_output, log_norms, grad_dots, block_routes, owner_steps
    ):
        tokens = queries.shape[0]
        features = key_states.shape[1]
        device = lax.axis_index("ctx")
        start = device * tokens
        steps = owner_steps.shape[0]
        is_mine = owner_steps == device
        covered = jnp.any(is_mine)
        kv = jnp.concatenate([key_states, value_states], axis=1)
        nz = n // 2
        sub = 16
        m = steps * tokens // (2 * nz * sub)
        per = 2 * nz // steps
        kv_all = grid_allreduce(
            kv.reshape(per, m, sub, 2 * features), 0,
            shape=(2, nz, m, sub, 2 * features), flags=is_mine.astype(jnp.int32),
        ).reshape(steps, tokens, 2 * features)
        listed = jnp.any(block_routes[0][None, :] == owner_steps[:, None], axis=1)
        remote = listed & (owner_steps != device) & (owner_steps < device)
        flags = jnp.concatenate([jnp.ones((1,), jnp.int32), remote.astype(jnp.int32)])
        grad_q, grad_k, grad_v, terms = pair_terms(
            flags, queries, grad_output, log_norms, grad_dots, key_states, value_states, kv_all
        )
        summed = slot_allreduce(terms, n, 1)
        held = lax.dynamic_index_in_dim(summed, jnp.argmax(is_mine), keepdims=False)
        held = jnp.where(covered, held, jnp.float32(0.0))
        grad_k = grad_k + held[:, :features]
        grad_v = grad_v + held[:, features:]
        return (grad_q, grad_k.astype(jnp.bfloat16), grad_v.astype(jnp.bfloat16))

    return on_device


def solution(mesh):
    n = mesh.shape["ctx"]
    return jax.shard_map(
        make_on_device(n),
        mesh=mesh,
        in_specs=(
            P(("dp", "ctx"), None),
            P(("dp", "ctx"), None),
            P(("dp", "ctx"), None),
            P(("dp", "ctx"), None),
            P(None, ("dp", "ctx")),
            P(None, ("dp", "ctx")),
            P(("dp", "ctx"), None),
            P("dp"),
        ),
        out_specs=(P(("dp", "ctx"), None), P(("dp", "ctx"), None), P(("dp", "ctx"), None)),
        check_vma=False,
    )
```

```python
import functools
import math

import jax
import jax.numpy as jnp
from jax import lax
from jax.experimental import pallas as pl
from jax.experimental.pallas import tpu as pltpu
from jax.sharding import PartitionSpec as P

HQ = 16
HK = 4
DH = 128
BLK = 256
MESH = pl.DeviceIdType.MESH


def grid_kernel(nz, m, n_in, *refs):
    ins = refs[:n_in]
    o_ref, rbuf, ybuf, rs_send, rs_recv, y_send, y_recv, ag_send, ag_recv, ready = refs[n_in:]
    me = lax.axis_index("ctx")
    row = lax.axis_index("dp")
    z = me // 2
    y = me % 2
    right = ((z + 1) % nz) * 2 + y
    left = ((z + nz - 1) % nz) * 2 + y
    partner = z * 2 + (1 - y)
    peers = (right, left)

    barrier = pltpu.get_barrier_semaphore()
    for nb in (left, right, partner):
        pl.semaphore_signal(barrier, inc=1, device_id=(row, nb), device_id_type=MESH)
    pl.semaphore_wait(barrier, 3)

    if n_in == 1:
        o_ref[...] = ins[0][...]
    else:
        flag_ref, kv_ref = ins
        per = kv_ref.shape[0]
        for i in range(flag_ref.shape[0]):
            d, c = divmod(i * per, nz)
            o_ref[d, c:c + per] = jnp.where(flag_ref[i] > 0, kv_ref[...], jnp.zeros((), kv_ref.dtype))

    def rs_copy(d, s, k):
        send = (z + nz - s) % nz if d == 0 else (z + s) % nz
        return pltpu.make_async_remote_copy(
            src_ref=o_ref.at[d, send, k],
            dst_ref=rbuf.at[d, s, k],
            send_sem=rs_send.at[d, s, k],
            recv_sem=rs_recv.at[d, s, k],
            device_id=(row, peers[d]),
            device_id_type=MESH,
        )

    for k in range(m):
        for d in range(2):
            rs_copy(d, 0, k).start()

    def rs_step(s, carry):
        for k in range(m):
            for d in range(2):
                rs_copy(d, s, k).wait_recv()
                got = (z + 2 * nz - s - 1) % nz if d == 0 else (z + s + 1) % nz
                o_ref[d, got, k] = o_ref[d, got, k] + rbuf[d, s, k]

                @pl.when(s < nz - 2)
                def _():
                    rs_copy(d, s + 1, k).start()

        return carry

    lax.fori_loop(0, nz - 1, rs_step, 0)

    mine = ((z + 1) % nz, (z + nz - 1) % nz)

    def y_copy(d, k):
        return pltpu.make_async_remote_copy(
            src_ref=o_ref.at[d, mine[d], k],
            dst_ref=ybuf.at[d, k],
            send_sem=y_send.at[d, k],
            recv_sem=y_recv.at[d, k],
            device_id=(row, partner),
            device_id_type=MESH,
        )

    for k in range(m):
        for d in range(2):
            y_copy(d, k).start()
    for k in range(m):
        for d in range(2):
            c = y_copy(d, k)
            c.wait_recv()
            c.wait_send()
            o_ref[d, mine[d], k] = o_ref[d, mine[d], k] + ybuf[d, k]

    def rs_drain(s, carry):
        for k in range(m):
            for d in range(2):
                rs_copy(d, s, k).wait_send()
        return carry

    lax.fori_loop(0, nz - 1, rs_drain, 0)
    for nb in (left, right):
        pl.semaphore_signal(ready, inc=1, device_id=(row, nb), device_id_type=MESH)
    pl.semaphore_wait(ready, 2)

    def ag_copy(d, t, k):
        chunk = (z + 1 + nz - t) % nz if d == 0 else (z + nz - 1 + t) % nz
        return pltpu.make_async_remote_copy(
            src_ref=o_ref.at[d, chunk, k],
            dst_ref=o_ref.at[d, chunk, k],
            send_sem=ag_send.at[d, t, k],
            recv_sem=ag_recv.at[d, t, k],
            device_id=(row, peers[d]),
            device_id_type=MESH,
        )

    for k in range(m):
        for d in range(2):
            ag_copy(d, 0, k).start()

    def ag_step(t, carry):
        for k in range(m):
            for d in range(2):
                ag_copy(d, t, k).wait_recv()

                @pl.when(t < nz - 2)
                def _():
                    ag_copy(d, t + 1, k).start()

        return carry

    lax.fori_loop(0, nz - 1, ag_step, 0)

    def drain(s, carry):
        for k in range(m):
            for d in range(2):
                ag_copy(d, s, k).wait_send()
        return carry

    lax.fori_loop(0, nz - 1, drain, 0)


def grid_allreduce(x, cid, shape=None, flags=None):
    shape = x.shape if shape is None else shape
    _, nz, m, rows, cols = shape
    ins = (x,) if flags is None else (flags, x)
    specs = [pl.BlockSpec(memory_space=pltpu.VMEM)]
    if flags is not None:
        specs = [pl.BlockSpec(memory_space=pltpu.SMEM)] + specs
    return pl.pallas_call(
        functools.partial(grid_kernel, nz, m, len(ins)),
        out_shape=jax.ShapeDtypeStruct(shape, x.dtype),
        in_specs=specs,
        out_specs=pl.BlockSpec(memory_space=pltpu.VMEM),
        scratch_shapes=[
            pltpu.VMEM((2, nz - 1, m, rows, cols), x.dtype),
            pltpu.VMEM((2, m, rows, cols), x.dtype),
            pltpu.SemaphoreType.DMA((2, nz - 1, m)),
            pltpu.SemaphoreType.DMA((2, nz - 1, m)),
            pltpu.SemaphoreType.DMA((2, m)),
            pltpu.SemaphoreType.DMA((2, m)),
            pltpu.SemaphoreType.DMA((2, nz - 1, m)),
            pltpu.SemaphoreType.DMA((2, nz - 1, m)),
            pltpu.SemaphoreType.REGULAR,
        ],
        compiler_params=pltpu.CompilerParams(collective_id=cid, has_side_effects=True),
    )(*ins)


def slot_allreduce(slots, n, cid):
    steps, rows, cols = slots.shape
    total = steps * rows
    sub = 16
    nz = n // 2
    m = total // (2 * nz * sub)
    out = grid_allreduce(slots.reshape(2, nz, m, sub, cols), cid)
    return out.reshape(steps, rows, cols)


def pair_kernel(scale, group, flag_ref, q_ref, do_ref, k_ref, v_ref, kv_ref, lse_ref, dot_ref,
                dq_ref, dk_ref, dv_ref, terms_ref, mask_ref):
    h = pl.program_id(0)
    g = h // group
    steps, tokens, width = kv_ref.shape
    features = width // 2

    @pl.when(h == 0)
    def _():
        key_pos = lax.broadcasted_iota(jnp.int32, (BLK, BLK), 0)
        query_pos = lax.broadcasted_iota(jnp.int32, (BLK, BLK), 1)
        mask_ref[0:BLK, :] = jnp.where(key_pos <= query_pos, jnp.float32(1.0), jnp.float32(0.0))
        for j in range(1, mask_ref.shape[0] // BLK):
            mask_ref[j * BLK:(j + 1) * BLK, :] = jnp.full(
                (BLK, mask_ref.shape[1]), flag_ref[j].astype(jnp.float32), jnp.float32
            )

    k_lane = pl.ds(pl.multiple_of(g * DH, DH), DH)
    v_lane = pl.ds(pl.multiple_of(features + g * DH, DH), DH)
    qh = q_ref[...]
    doh = do_ref[...]
    kg = jnp.concatenate([k_ref[...], kv_ref[:, :, k_lane].reshape(steps * tokens, DH)], axis=0)
    vg = jnp.concatenate([v_ref[...], kv_ref[:, :, v_lane].reshape(steps * tokens, DH)], axis=0)
    nt = (((1,), (1,)), ((), ()))
    scores = lax.dot_general(kg, qh, nt, preferred_element_type=jnp.float32) * scale
    lse = lse_ref[pl.ds(h, 1), :]
    dots = dot_ref[pl.ds(h, 1), :]
    probs = jnp.where(mask_ref[...] > 0, jnp.exp(scores - lse), jnp.float32(0.0))
    grad_probs = lax.dot_general(vg, doh, nt, preferred_element_type=jnp.float32)
    grad_scores = (probs * (grad_probs - dots)).astype(jnp.bfloat16)
    probs_low = probs.astype(jnp.bfloat16)
    tn = (((0,), (0,)), ((), ()))
    dq = lax.dot_general(grad_scores, kg, tn, preferred_element_type=jnp.float32) * scale
    dq_ref[...] = dq.astype(dq_ref.dtype)
    dk = jnp.dot(grad_scores, qh, preferred_element_type=jnp.float32) * scale
    dv = jnp.dot(probs_low, doh, preferred_element_type=jnp.float32)
    dk_far = dk[tokens:].reshape(steps, tokens, DH)
    dv_far = dv[tokens:].reshape(steps, tokens, DH)

    @pl.when(h % group == 0)
    def _():
        dk_ref[...] = dk[:tokens]
        dv_ref[...] = dv[:tokens]
        terms_ref[:, :, k_lane] = dk_far
        terms_ref[:, :, v_lane] = dv_far

    @pl.when(h % group != 0)
    def _():
        dk_ref[...] += dk[:tokens]
        dv_ref[...] += dv[:tokens]
        terms_ref[:, :, k_lane] += dk_far
        terms_ref[:, :, v_lane] += dv_far


def pair_terms(flags, query_rows, grad_rows, norm_rows, dot_rows, key_rows, value_rows, kv_all):
    rows = query_rows.shape[0]
    tokens = key_rows.shape[0]
    steps, _, width = kv_all.shape
    cols = tokens * (1 + steps)
    group = HQ // HK
    scale = 1.0 / math.sqrt(DH)
    return pl.pallas_call(
        functools.partial(pair_kernel, scale, group),
        out_shape=(
            jax.ShapeDtypeStruct((rows, HQ * DH), jnp.bfloat16),
            jax.ShapeDtypeStruct((tokens, HK * DH), jnp.float32),
            jax.ShapeDtypeStruct((tokens, HK * DH), jnp.float32),
            jax.ShapeDtypeStruct((steps, tokens, width), jnp.float32),
        ),
        grid=(HQ,),
        in_specs=[
            pl.BlockSpec(memory_space=pltpu.SMEM),
            pl.BlockSpec((rows, DH), lambda h: (0, h)),
            pl.BlockSpec((rows, DH), lambda h: (0, h)),
            pl.BlockSpec((tokens, DH), lambda h: (0, h // group)),
            pl.BlockSpec((tokens, DH), lambda h: (0, h // group)),
            pl.BlockSpec((steps, tokens, width), lambda h: (0, 0, 0)),
            pl.BlockSpec((HQ, rows), lambda h: (0, 0)),
            pl.BlockSpec((HQ, rows), lambda h: (0, 0)),
        ],
        out_specs=[
            pl.BlockSpec((rows, DH), lambda h: (0, h)),
            pl.BlockSpec((tokens, DH), lambda h: (0, h // group)),
            pl.BlockSpec((tokens, DH), lambda h: (0, h // group)),
            pl.BlockSpec((steps, tokens, width), lambda h: (0, 0, 0)),
        ],
        scratch_shapes=[pltpu.VMEM((cols, rows), jnp.float32)],
        compiler_params=pltpu.CompilerParams(dimension_semantics=("arbitrary",)),
    )(flags, query_rows, grad_rows, key_rows, value_rows, kv_all, norm_rows, dot_rows)


def allowed_rows(local_routes, query_start, key_start, tokens, widen, active):
    per_dev = local_routes.shape[0]
    query_blocks = query_start // BLK + jnp.arange(per_dev, dtype=jnp.int32)
    key_blocks = key_start // BLK + jnp.arange(per_dev, dtype=jnp.int32)
    listed = jnp.any(local_routes[:, :, None] == key_blocks[None, None, :], axis=1)
    same = query_blocks[:, None] == key_blocks[None, :]
    chosen = listed & (same | widen) & active
    token_level = jnp.broadcast_to(chosen[:, None, :, None], (per_dev, BLK, per_dev, BLK)).reshape(
        tokens, tokens
    )
    positions = jnp.arange(tokens, dtype=jnp.int32)
    causal = key_start + positions[None, :] <= query_start + positions[:, None]
    return token_level & causal


def make_on_device(n):
    def on_device(
        queries, key_states, value_states, grad_output, log_norms, grad_dots, block_routes, owner_steps
    ):
        tokens = queries.shape[0]
        features = key_states.shape[1]
        device = lax.axis_index("ctx")
        start = device * tokens
        steps = owner_steps.shape[0]
        is_mine = owner_steps == device
        covered = jnp.any(is_mine)
        kv = jnp.concatenate([key_states, value_states], axis=1)
        nz = n // 2
        sub = 16
        m = steps * tokens // (2 * nz * sub)
        per = 2 * nz // steps
        kv_all = grid_allreduce(
            kv.reshape(per, m, sub, 2 * features), 0,
            shape=(2, nz, m, sub, 2 * features), flags=is_mine.astype(jnp.int32),
        ).reshape(steps, tokens, 2 * features)
        listed = jnp.any(block_routes[0][None, :] == owner_steps[:, None], axis=1)
        remote = listed & (owner_steps != device) & (owner_steps < device)
        flags = jnp.concatenate([jnp.ones((1,), jnp.int32), remote.astype(jnp.int32)])
        grad_q, grad_k, grad_v, terms = pair_terms(
            flags, queries, grad_output, log_norms, grad_dots, key_states, value_states, kv_all
        )
        summed = slot_allreduce(terms, n, 1)
        held = lax.dynamic_index_in_dim(summed, jnp.argmax(is_mine), keepdims=False)
        held = jnp.where(covered, held, jnp.float32(0.0))
        grad_k = grad_k + held[:, :features]
        grad_v = grad_v + held[:, features:]
        return (grad_q, grad_k.astype(jnp.bfloat16), grad_v.astype(jnp.bfloat16))

    return on_device


def solution(mesh):
    n = mesh.shape["ctx"]
    return jax.shard_map(
        make_on_device(n),
        mesh=mesh,
        in_specs=(
            P(("dp", "ctx"), None),
            P(("dp", "ctx"), None),
            P(("dp", "ctx"), None),
            P(("dp", "ctx"), None),
            P(None, ("dp", "ctx")),
            P(None, ("dp", "ctx")),
            P(("dp", "ctx"), None),
            P("dp"),
        ),
        out_specs=(P(("dp", "ctx"), None), P(("dp", "ctx"), None), P(("dp", "ctx"), None)),
        check_vma=False,
    )
```

```python
import functools
import math

import jax
import jax.numpy as jnp
from jax import lax
from jax.experimental import pallas as pl
from jax.experimental.pallas import tpu as pltpu
from jax.sharding import PartitionSpec as P

HQ = 16
HK = 4
DH = 128
BLK = 256
MESH = pl.DeviceIdType.MESH


def grid_kernel(nz, m, n_in, *refs):
    ins = refs[:n_in]
    o_ref, rbuf, ybuf, rs_send, rs_recv, y_send, y_recv, ag_send, ag_recv, ready = refs[n_in:]
    me = lax.axis_index("ctx")
    row = lax.axis_index("dp")
    z = me // 2
    y = me % 2
    right = ((z + 1) % nz) * 2 + y
    left = ((z + nz - 1) % nz) * 2 + y
    partner = z * 2 + (1 - y)
    peers = (right, left)

    barrier = pltpu.get_barrier_semaphore()
    for nb in (left, right, partner):
        pl.semaphore_signal(barrier, inc=1, device_id=(row, nb), device_id_type=MESH)
    pl.semaphore_wait(barrier, 3)

    if n_in == 1:
        o_ref[...] = ins[0][...]
    else:
        flag_ref, k_ref, v_ref = ins
        per = k_ref.shape[0]
        half = k_ref.shape[-1]
        zero = jnp.zeros((), k_ref.dtype)
        for i in range(flag_ref.shape[0]):
            d, c = divmod(i * per, nz)
            o_ref[d, c:c + per, :, :, :half] = jnp.where(flag_ref[i] > 0, k_ref[...], zero)
            o_ref[d, c:c + per, :, :, half:] = jnp.where(flag_ref[i] > 0, v_ref[...], zero)

    def rs_copy(d, s, k):
        send = (z + nz - s) % nz if d == 0 else (z + s) % nz
        return pltpu.make_async_remote_copy(
            src_ref=o_ref.at[d, send, k],
            dst_ref=rbuf.at[d, s, k],
            send_sem=rs_send.at[d, s, k],
            recv_sem=rs_recv.at[d, s, k],
            device_id=(row, peers[d]),
            device_id_type=MESH,
        )

    for k in range(m):
        for d in range(2):
            rs_copy(d, 0, k).start()

    def rs_step(s, carry):
        for k in range(m):
            for d in range(2):
                rs_copy(d, s, k).wait_recv()
                got = (z + 2 * nz - s - 1) % nz if d == 0 else (z + s + 1) % nz
                o_ref[d, got, k] = o_ref[d, got, k] + rbuf[d, s, k]

                @pl.when(s < nz - 2)
                def _():
                    rs_copy(d, s + 1, k).start()

        return carry

    lax.fori_loop(0, nz - 1, rs_step, 0)

    mine = ((z + 1) % nz, (z + nz - 1) % nz)

    def y_copy(d, k):
        return pltpu.make_async_remote_copy(
            src_ref=o_ref.at[d, mine[d], k],
            dst_ref=ybuf.at[d, k],
            send_sem=y_send.at[d, k],
            recv_sem=y_recv.at[d, k],
            device_id=(row, partner),
            device_id_type=MESH,
        )

    for k in range(m):
        for d in range(2):
            y_copy(d, k).start()
    for k in range(m):
        for d in range(2):
            c = y_copy(d, k)
            c.wait_recv()
            c.wait_send()
            o_ref[d, mine[d], k] = o_ref[d, mine[d], k] + ybuf[d, k]

    def rs_drain(s, carry):
        for k in range(m):
            for d in range(2):
                rs_copy(d, s, k).wait_send()
        return carry

    lax.fori_loop(0, nz - 1, rs_drain, 0)
    for nb in (left, right):
        pl.semaphore_signal(ready, inc=1, device_id=(row, nb), device_id_type=MESH)
    pl.semaphore_wait(ready, 2)

    def ag_copy(d, t, k):
        chunk = (z + 1 + nz - t) % nz if d == 0 else (z + nz - 1 + t) % nz
        return pltpu.make_async_remote_copy(
            src_ref=o_ref.at[d, chunk, k],
            dst_ref=o_ref.at[d, chunk, k],
            send_sem=ag_send.at[d, t, k],
            recv_sem=ag_recv.at[d, t, k],
            device_id=(row, peers[d]),
            device_id_type=MESH,
        )

    for k in range(m):
        for d in range(2):
            ag_copy(d, 0, k).start()

    def ag_step(t, carry):
        for k in range(m):
            for d in range(2):
                ag_copy(d, t, k).wait_recv()

                @pl.when(t < nz - 2)
                def _():
                    ag_copy(d, t + 1, k).start()

        return carry

    lax.fori_loop(0, nz - 1, ag_step, 0)

    def drain(s, carry):
        for k in range(m):
            for d in range(2):
                ag_copy(d, s, k).wait_send()
        return carry

    lax.fori_loop(0, nz - 1, drain, 0)


def grid_allreduce(x, cid, shape=None, flags=None, extra=()):
    shape = x.shape if shape is None else shape
    _, nz, m, rows, cols = shape
    ins = (x,) + tuple(extra) if flags is None else (flags, x) + tuple(extra)
    specs = [pl.BlockSpec(memory_space=pltpu.VMEM)] * (1 + len(extra))
    if flags is not None:
        specs = [pl.BlockSpec(memory_space=pltpu.SMEM)] + specs
    return pl.pallas_call(
        functools.partial(grid_kernel, nz, m, len(ins)),
        out_shape=jax.ShapeDtypeStruct(shape, x.dtype),
        in_specs=specs,
        out_specs=pl.BlockSpec(memory_space=pltpu.VMEM),
        scratch_shapes=[
            pltpu.VMEM((2, nz - 1, m, rows, cols), x.dtype),
            pltpu.VMEM((2, m, rows, cols), x.dtype),
            pltpu.SemaphoreType.DMA((2, nz - 1, m)),
            pltpu.SemaphoreType.DMA((2, nz - 1, m)),
            pltpu.SemaphoreType.DMA((2, m)),
            pltpu.SemaphoreType.DMA((2, m)),
            pltpu.SemaphoreType.DMA((2, nz - 1, m)),
            pltpu.SemaphoreType.DMA((2, nz - 1, m)),
            pltpu.SemaphoreType.REGULAR,
        ],
        compiler_params=pltpu.CompilerParams(collective_id=cid, has_side_effects=True),
    )(*ins)


def slot_allreduce(slots, n, cid):
    steps, rows, cols = slots.shape
    total = steps * rows
    sub = 16 if slots.dtype == jnp.bfloat16 else 8
    nz = n // 2
    m = total // (2 * nz * sub)
    out = grid_allreduce(slots.reshape(2, nz, m, sub, cols), cid)
    return out.reshape(steps, rows, cols)


def pair_kernel(scale, group, flag_ref, q_ref, do_ref, k_ref, v_ref, kv_ref, lse_ref, dot_ref,
                dq_ref, dk_ref, dv_ref, terms_ref, mask_ref):
    h = pl.program_id(0)
    g = h // group
    steps, tokens, width = kv_ref.shape
    features = width // 2

    @pl.when(h == 0)
    def _():
        key_pos = lax.broadcasted_iota(jnp.int32, (BLK, BLK), 0)
        query_pos = lax.broadcasted_iota(jnp.int32, (BLK, BLK), 1)
        mask_ref[0:BLK, :] = jnp.where(key_pos <= query_pos, jnp.float32(1.0), jnp.float32(0.0))
        for j in range(1, mask_ref.shape[0] // BLK):
            mask_ref[j * BLK:(j + 1) * BLK, :] = jnp.full(
                (BLK, mask_ref.shape[1]), flag_ref[j].astype(jnp.float32), jnp.float32
            )

    k_lane = pl.ds(pl.multiple_of(g * DH, DH), DH)
    v_lane = pl.ds(pl.multiple_of(features + g * DH, DH), DH)
    qh = q_ref[...]
    doh = do_ref[...]
    kg = jnp.concatenate([k_ref[...], kv_ref[:, :, k_lane].reshape(steps * tokens, DH)], axis=0)
    vg = jnp.concatenate([v_ref[...], kv_ref[:, :, v_lane].reshape(steps * tokens, DH)], axis=0)
    nt = (((1,), (1,)), ((), ()))
    scores = lax.dot_general(kg, qh, nt, preferred_element_type=jnp.float32) * scale
    lse = lse_ref[pl.ds(h, 1), :]
    dots = dot_ref[pl.ds(h, 1), :]
    probs = jnp.where(mask_ref[...] > 0, jnp.exp(scores - lse), jnp.float32(0.0))
    grad_probs = lax.dot_general(vg, doh, nt, preferred_element_type=jnp.float32)
    grad_scores = (probs * (grad_probs - dots)).astype(jnp.bfloat16)
    probs_low = probs.astype(jnp.bfloat16)
    tn = (((0,), (0,)), ((), ()))
    dq = lax.dot_general(grad_scores, kg, tn, preferred_element_type=jnp.float32) * scale
    dq_ref[...] = dq.astype(dq_ref.dtype)
    dk = jnp.dot(grad_scores, qh, preferred_element_type=jnp.float32) * scale
    dv = jnp.dot(probs_low, doh, preferred_element_type=jnp.float32)
    dk_far = dk[tokens:].reshape(steps, tokens, DH)
    dv_far = dv[tokens:].reshape(steps, tokens, DH)

    @pl.when(h % group == 0)
    def _():
        dk_ref[...] = dk[:tokens]
        dv_ref[...] = dv[:tokens]
        terms_ref[:, :, k_lane] = dk_far
        terms_ref[:, :, v_lane] = dv_far

    @pl.when(h % group != 0)
    def _():
        dk_ref[...] += dk[:tokens]
        dv_ref[...] += dv[:tokens]
        terms_ref[:, :, k_lane] += dk_far
        terms_ref[:, :, v_lane] += dv_far


def pair_terms(flags, query_rows, grad_rows, norm_rows, dot_rows, key_rows, value_rows, kv_all):
    rows = query_rows.shape[0]
    tokens = key_rows.shape[0]
    steps, _, width = kv_all.shape
    cols = tokens * (1 + steps)
    group = HQ // HK
    scale = 1.0 / math.sqrt(DH)
    return pl.pallas_call(
        functools.partial(pair_kernel, scale, group),
        out_shape=(
            jax.ShapeDtypeStruct((rows, HQ * DH), jnp.bfloat16),
            jax.ShapeDtypeStruct((tokens, HK * DH), jnp.float32),
            jax.ShapeDtypeStruct((tokens, HK * DH), jnp.float32),
            jax.ShapeDtypeStruct((steps, tokens, width), jnp.float32),
        ),
        grid=(HQ,),
        in_specs=[
            pl.BlockSpec(memory_space=pltpu.SMEM),
            pl.BlockSpec((rows, DH), lambda h: (0, h)),
            pl.BlockSpec((rows, DH), lambda h: (0, h)),
            pl.BlockSpec((tokens, DH), lambda h: (0, h // group)),
            pl.BlockSpec((tokens, DH), lambda h: (0, h // group)),
            pl.BlockSpec((steps, tokens, width), lambda h: (0, 0, 0)),
            pl.BlockSpec((HQ, rows), lambda h: (0, 0)),
            pl.BlockSpec((HQ, rows), lambda h: (0, 0)),
        ],
        out_specs=[
            pl.BlockSpec((rows, DH), lambda h: (0, h)),
            pl.BlockSpec((tokens, DH), lambda h: (0, h // group)),
            pl.BlockSpec((tokens, DH), lambda h: (0, h // group)),
            pl.BlockSpec((steps, tokens, width), lambda h: (0, 0, 0)),
        ],
        scratch_shapes=[pltpu.VMEM((cols, rows), jnp.float32)],
        compiler_params=pltpu.CompilerParams(dimension_semantics=("arbitrary",)),
    )(flags, query_rows, grad_rows, key_rows, value_rows, kv_all, norm_rows, dot_rows)


def allowed_rows(local_routes, query_start, key_start, tokens, widen, active):
    per_dev = local_routes.shape[0]
    query_blocks = query_start // BLK + jnp.arange(per_dev, dtype=jnp.int32)
    key_blocks = key_start // BLK + jnp.arange(per_dev, dtype=jnp.int32)
    listed = jnp.any(local_routes[:, :, None] == key_blocks[None, None, :], axis=1)
    same = query_blocks[:, None] == key_blocks[None, :]
    chosen = listed & (same | widen) & active
    token_level = jnp.broadcast_to(chosen[:, None, :, None], (per_dev, BLK, per_dev, BLK)).reshape(
        tokens, tokens
    )
    positions = jnp.arange(tokens, dtype=jnp.int32)
    causal = key_start + positions[None, :] <= query_start + positions[:, None]
    return token_level & causal


def make_on_device(n):
    def on_device(
        queries, key_states, value_states, grad_output, log_norms, grad_dots, block_routes, owner_steps
    ):
        tokens = queries.shape[0]
        features = key_states.shape[1]
        device = lax.axis_index("ctx")
        start = device * tokens
        steps = owner_steps.shape[0]
        is_mine = owner_steps == device
        covered = jnp.any(is_mine)
        nz = n // 2
        sub = 16
        m = steps * tokens // (2 * nz * sub)
        per = 2 * nz // steps
        kv_all = grid_allreduce(
            key_states.reshape(per, m, sub, features), 0,
            shape=(2, nz, m, sub, 2 * features), flags=is_mine.astype(jnp.int32),
            extra=(value_states.reshape(per, m, sub, features),),
        ).reshape(steps, tokens, 2 * features)
        listed = jnp.any(block_routes[0][None, :] == owner_steps[:, None], axis=1)
        remote = listed & (owner_steps != device) & (owner_steps < device)
        flags = jnp.concatenate([jnp.ones((1,), jnp.int32), remote.astype(jnp.int32)])
        grad_q, grad_k, grad_v, terms = pair_terms(
            flags, queries, grad_output, log_norms, grad_dots, key_states, value_states, kv_all
        )
        summed = slot_allreduce(terms, n, 1)
        held = lax.dynamic_index_in_dim(summed, jnp.argmax(is_mine), keepdims=False)
        held = jnp.where(covered, held, jnp.float32(0.0))
        grad_k = grad_k + held[:, :features]
        grad_v = grad_v + held[:, features:]
        return (grad_q, grad_k.astype(jnp.bfloat16), grad_v.astype(jnp.bfloat16))

    return on_device


def solution(mesh):
    n = mesh.shape["ctx"]
    return jax.shard_map(
        make_on_device(n),
        mesh=mesh,
        in_specs=(
            P(("dp", "ctx"), None),
            P(("dp", "ctx"), None),
            P(("dp", "ctx"), None),
            P(("dp", "ctx"), None),
            P(None, ("dp", "ctx")),
            P(None, ("dp", "ctx")),
            P(("dp", "ctx"), None),
            P("dp"),
        ),
        out_specs=(P(("dp", "ctx"), None), P(("dp", "ctx"), None), P(("dp", "ctx"), None)),
        check_vma=False,
    )
```

```python
import functools
import math

import jax
import jax.numpy as jnp
from jax import lax
from jax.experimental import pallas as pl
from jax.experimental.pallas import tpu as pltpu
from jax.sharding import PartitionSpec as P

HQ = 16
HK = 4
DH = 128
BLK = 256
MESH = pl.DeviceIdType.MESH


def grid_kernel(nz, m, n_in, *refs):
    ins = refs[:n_in]
    o_ref, rbuf, ybuf, rs_send, rs_recv, y_send, y_recv, ag_send, ag_recv, ready = refs[n_in:]
    me = lax.axis_index("ctx")
    row = lax.axis_index("dp")
    z = me // 2
    y = me % 2
    right = ((z + 1) % nz) * 2 + y
    left = ((z + nz - 1) % nz) * 2 + y
    partner = z * 2 + (1 - y)
    peers = (right, left)

    barrier = pltpu.get_barrier_semaphore()
    for nb in (left, right, partner):
        pl.semaphore_signal(barrier, inc=1, device_id=(row, nb), device_id_type=MESH)
    pl.semaphore_wait(barrier, 3)

    if n_in == 1:
        o_ref[...] = ins[0][...]
    else:
        flag_ref, k_ref, v_ref = ins
        per = k_ref.shape[0]
        half = k_ref.shape[-1]
        zero = jnp.zeros((), k_ref.dtype)
        for i in range(flag_ref.shape[0]):
            d, c = divmod(i * per, nz)
            o_ref[d, c:c + per, :, :, :half] = jnp.where(flag_ref[i] > 0, k_ref[...], zero)
            o_ref[d, c:c + per, :, :, half:] = jnp.where(flag_ref[i] > 0, v_ref[...], zero)

    def rs_copy(d, s, k):
        send = (z + nz - s) % nz if d == 0 else (z + s) % nz
        return pltpu.make_async_remote_copy(
            src_ref=o_ref.at[d, send, k],
            dst_ref=rbuf.at[d, s, k],
            send_sem=rs_send.at[d, s, k],
            recv_sem=rs_recv.at[d, s, k],
            device_id=(row, peers[d]),
            device_id_type=MESH,
        )

    for k in range(m):
        for d in range(2):
            rs_copy(d, 0, k).start()

    def rs_step(s, carry):
        for k in range(m):
            for d in range(2):
                rs_copy(d, s, k).wait_recv()
                got = (z + 2 * nz - s - 1) % nz if d == 0 else (z + s + 1) % nz
                o_ref[d, got, k] = o_ref[d, got, k] + rbuf[d, s, k]

                @pl.when(s < nz - 2)
                def _():
                    rs_copy(d, s + 1, k).start()

        return carry

    lax.fori_loop(0, nz - 1, rs_step, 0)

    mine = ((z + 1) % nz, (z + nz - 1) % nz)

    def y_copy(d, k):
        return pltpu.make_async_remote_copy(
            src_ref=o_ref.at[d, mine[d], k],
            dst_ref=ybuf.at[d, k],
            send_sem=y_send.at[d, k],
            recv_sem=y_recv.at[d, k],
            device_id=(row, partner),
            device_id_type=MESH,
        )

    for k in range(m):
        for d in range(2):
            y_copy(d, k).start()
    for k in range(m):
        for d in range(2):
            c = y_copy(d, k)
            c.wait_recv()
            c.wait_send()
            o_ref[d, mine[d], k] = o_ref[d, mine[d], k] + ybuf[d, k]

    def rs_drain(s, carry):
        for k in range(m):
            for d in range(2):
                rs_copy(d, s, k).wait_send()
        return carry

    lax.fori_loop(0, nz - 1, rs_drain, 0)
    for nb in (left, right):
        pl.semaphore_signal(ready, inc=1, device_id=(row, nb), device_id_type=MESH)
    pl.semaphore_wait(ready, 2)

    def ag_copy(d, t, k):
        chunk = (z + 1 + nz - t) % nz if d == 0 else (z + nz - 1 + t) % nz
        return pltpu.make_async_remote_copy(
            src_ref=o_ref.at[d, chunk, k],
            dst_ref=o_ref.at[d, chunk, k],
            send_sem=ag_send.at[d, t, k],
            recv_sem=ag_recv.at[d, t, k],
            device_id=(row, peers[d]),
            device_id_type=MESH,
        )

    for k in range(m):
        for d in range(2):
            ag_copy(d, 0, k).start()

    def ag_step(t, carry):
        for k in range(m):
            for d in range(2):
                ag_copy(d, t, k).wait_recv()

                @pl.when(t < nz - 2)
                def _():
                    ag_copy(d, t + 1, k).start()

        return carry

    lax.fori_loop(0, nz - 1, ag_step, 0)

    def drain(s, carry):
        for k in range(m):
            for d in range(2):
                ag_copy(d, s, k).wait_send()
        return carry

    lax.fori_loop(0, nz - 1, drain, 0)


def grid_allreduce(x, cid, shape=None, flags=None, extra=()):
    shape = x.shape if shape is None else shape
    _, nz, m, rows, cols = shape
    ins = (x,) + tuple(extra) if flags is None else (flags, x) + tuple(extra)
    specs = [pl.BlockSpec(memory_space=pltpu.VMEM)] * (1 + len(extra))
    if flags is not None:
        specs = [pl.BlockSpec(memory_space=pltpu.SMEM)] + specs
    return pl.pallas_call(
        functools.partial(grid_kernel, nz, m, len(ins)),
        out_shape=jax.ShapeDtypeStruct(shape, x.dtype),
        in_specs=specs,
        out_specs=pl.BlockSpec(memory_space=pltpu.VMEM),
        scratch_shapes=[
            pltpu.VMEM((2, nz - 1, m, rows, cols), x.dtype),
            pltpu.VMEM((2, m, rows, cols), x.dtype),
            pltpu.SemaphoreType.DMA((2, nz - 1, m)),
            pltpu.SemaphoreType.DMA((2, nz - 1, m)),
            pltpu.SemaphoreType.DMA((2, m)),
            pltpu.SemaphoreType.DMA((2, m)),
            pltpu.SemaphoreType.DMA((2, nz - 1, m)),
            pltpu.SemaphoreType.DMA((2, nz - 1, m)),
            pltpu.SemaphoreType.REGULAR,
        ],
        compiler_params=pltpu.CompilerParams(collective_id=cid, has_side_effects=True),
    )(*ins)


def slot_allreduce(slots, n, cid):
    steps, rows, cols = slots.shape
    total = steps * rows
    sub = 16 if slots.dtype == jnp.bfloat16 else 8
    nz = n // 2
    m = total // (2 * nz * sub)
    out = grid_allreduce(slots.reshape(2, nz, m, sub, cols), cid)
    return out.reshape(steps, rows, cols)


def pair_kernel(scale, group, flag_ref, q_ref, do_ref, k_ref, v_ref, kv_ref, lse_ref, dot_ref,
                dq_ref, dk_ref, dv_ref, terms_ref, mask_ref):
    h = pl.program_id(0)
    g = h // group
    steps, tokens, width = kv_ref.shape
    features = width // 2

    @pl.when(h == 0)
    def _():
        key_pos = lax.broadcasted_iota(jnp.int32, (BLK, BLK), 0)
        query_pos = lax.broadcasted_iota(jnp.int32, (BLK, BLK), 1)
        mask_ref[0:BLK, :] = jnp.where(key_pos <= query_pos, jnp.float32(1.0), jnp.float32(0.0))
        for j in range(1, mask_ref.shape[0] // BLK):
            mask_ref[j * BLK:(j + 1) * BLK, :] = jnp.full(
                (BLK, mask_ref.shape[1]), flag_ref[j].astype(jnp.float32), jnp.float32
            )

    k_lane = pl.ds(pl.multiple_of(g * DH, DH), DH)
    v_lane = pl.ds(pl.multiple_of(features + g * DH, DH), DH)
    qh = q_ref[...]
    doh = do_ref[...]
    kg = jnp.concatenate([k_ref[...], kv_ref[:, :, k_lane].reshape(steps * tokens, DH)], axis=0)
    vg = jnp.concatenate([v_ref[...], kv_ref[:, :, v_lane].reshape(steps * tokens, DH)], axis=0)
    nt = (((1,), (1,)), ((), ()))
    scores = lax.dot_general(kg, qh, nt, preferred_element_type=jnp.float32) * scale
    lse = lse_ref[pl.ds(h, 1), :]
    dots = dot_ref[pl.ds(h, 1), :]
    probs = jnp.where(mask_ref[...] > 0, jnp.exp(scores - lse), jnp.float32(0.0))
    grad_probs = lax.dot_general(vg, doh, nt, preferred_element_type=jnp.float32)
    grad_scores = (probs * (grad_probs - dots)).astype(jnp.bfloat16)
    probs_low = probs.astype(jnp.bfloat16)
    tn = (((0,), (0,)), ((), ()))
    dq = lax.dot_general(grad_scores, kg, tn, preferred_element_type=jnp.float32) * scale
    dq_ref[...] = dq.astype(dq_ref.dtype)
    dk = jnp.dot(grad_scores, qh, preferred_element_type=jnp.float32) * scale
    dv = jnp.dot(probs_low, doh, preferred_element_type=jnp.float32)
    dk_far = dk[tokens:].reshape(steps, tokens, DH)
    dv_far = dv[tokens:].reshape(steps, tokens, DH)

    @pl.when(h % group == 0)
    def _():
        dk_ref[...] = dk[:tokens]
        dv_ref[...] = dv[:tokens]
        terms_ref[:, :, k_lane] = dk_far
        terms_ref[:, :, v_lane] = dv_far

    @pl.when(h % group != 0)
    def _():
        dk_ref[...] += dk[:tokens]
        dv_ref[...] += dv[:tokens]
        terms_ref[:, :, k_lane] += dk_far
        terms_ref[:, :, v_lane] += dv_far


def pair_terms(flags, query_rows, grad_rows, norm_rows, dot_rows, key_rows, value_rows, kv_all):
    rows = query_rows.shape[0]
    tokens = key_rows.shape[0]
    steps, _, width = kv_all.shape
    cols = tokens * (1 + steps)
    group = HQ // HK
    scale = 1.0 / math.sqrt(DH)
    return pl.pallas_call(
        functools.partial(pair_kernel, scale, group),
        out_shape=(
            jax.ShapeDtypeStruct((rows, HQ * DH), jnp.bfloat16),
            jax.ShapeDtypeStruct((tokens, HK * DH), jnp.float32),
            jax.ShapeDtypeStruct((tokens, HK * DH), jnp.float32),
            jax.ShapeDtypeStruct((steps, tokens, width), jnp.float32),
        ),
        grid=(HQ,),
        in_specs=[
            pl.BlockSpec(memory_space=pltpu.SMEM),
            pl.BlockSpec((rows, DH), lambda h: (0, h)),
            pl.BlockSpec((rows, DH), lambda h: (0, h)),
            pl.BlockSpec((tokens, DH), lambda h: (0, h // group)),
            pl.BlockSpec((tokens, DH), lambda h: (0, h // group)),
            pl.BlockSpec((steps, tokens, width), lambda h: (0, 0, 0)),
            pl.BlockSpec((HQ, rows), lambda h: (0, 0)),
            pl.BlockSpec((HQ, rows), lambda h: (0, 0)),
        ],
        out_specs=[
            pl.BlockSpec((rows, DH), lambda h: (0, h)),
            pl.BlockSpec((tokens, DH), lambda h: (0, h // group)),
            pl.BlockSpec((tokens, DH), lambda h: (0, h // group)),
            pl.BlockSpec((steps, tokens, width), lambda h: (0, 0, 0)),
        ],
        scratch_shapes=[pltpu.VMEM((cols, rows), jnp.float32)],
        compiler_params=pltpu.CompilerParams(dimension_semantics=("arbitrary",)),
    )(flags, query_rows, grad_rows, key_rows, value_rows, kv_all, norm_rows, dot_rows)


def allowed_rows(local_routes, query_start, key_start, tokens, widen, active):
    per_dev = local_routes.shape[0]
    query_blocks = query_start // BLK + jnp.arange(per_dev, dtype=jnp.int32)
    key_blocks = key_start // BLK + jnp.arange(per_dev, dtype=jnp.int32)
    listed = jnp.any(local_routes[:, :, None] == key_blocks[None, None, :], axis=1)
    same = query_blocks[:, None] == key_blocks[None, :]
    chosen = listed & (same | widen) & active
    token_level = jnp.broadcast_to(chosen[:, None, :, None], (per_dev, BLK, per_dev, BLK)).reshape(
        tokens, tokens
    )
    positions = jnp.arange(tokens, dtype=jnp.int32)
    causal = key_start + positions[None, :] <= query_start + positions[:, None]
    return token_level & causal


def make_on_device(n):
    def on_device(
        queries, key_states, value_states, grad_output, log_norms, grad_dots, block_routes, owner_steps
    ):
        tokens = queries.shape[0]
        features = key_states.shape[1]
        device = lax.axis_index("ctx")
        start = device * tokens
        steps = owner_steps.shape[0]
        is_mine = owner_steps == device
        covered = jnp.any(is_mine)
        nz = n // 2
        sub = 16
        m = steps * tokens // (2 * nz * sub)
        per = 2 * nz // steps
        kv_all = grid_allreduce(
            key_states.reshape(per, m, sub, features), 0,
            shape=(2, nz, m, sub, 2 * features), flags=is_mine.astype(jnp.int32),
            extra=(value_states.reshape(per, m, sub, features),),
        ).reshape(steps, tokens, 2 * features)
        listed = jnp.any(block_routes[0][None, :] == owner_steps[:, None], axis=1)
        remote = listed & (owner_steps != device) & (owner_steps < device)
        flags = jnp.concatenate([jnp.ones((1,), jnp.int32), remote.astype(jnp.int32)])
        grad_q, grad_k, grad_v, terms = pair_terms(
            flags, queries, grad_output, log_norms, grad_dots, key_states, value_states, kv_all
        )
        summed = slot_allreduce(terms, n, 1)
        owned = jnp.sum(jnp.where(is_mine, jnp.arange(steps, dtype=jnp.int32), 0))
        held = lax.dynamic_index_in_dim(summed, owned, keepdims=False)
        held = jnp.where(covered, held, jnp.float32(0.0))
        grad_k = grad_k + held[:, :features]
        grad_v = grad_v + held[:, features:]
        return (grad_q, grad_k.astype(jnp.bfloat16), grad_v.astype(jnp.bfloat16))

    return on_device


def solution(mesh):
    n = mesh.shape["ctx"]
    return jax.shard_map(
        make_on_device(n),
        mesh=mesh,
        in_specs=(
            P(("dp", "ctx"), None),
            P(("dp", "ctx"), None),
            P(("dp", "ctx"), None),
            P(("dp", "ctx"), None),
            P(None, ("dp", "ctx")),
            P(None, ("dp", "ctx")),
            P(("dp", "ctx"), None),
            P("dp"),
        ),
        out_specs=(P(("dp", "ctx"), None), P(("dp", "ctx"), None), P(("dp", "ctx"), None)),
        check_vma=False,
    )
```
